256 devices in a mesh: shard: 32 (over y, z), blk: 8 (over x, core).
Axes of the slice: x: 4, y: 4, z: 8, core: 2. Of those that a mesh axis runs over, the one named last changes fastest.
Arguments:
- request_embeddings: bfloat16 [65536, 256], P(('shard', 'blk')), may hold values from -0.5 to 0.5
- frequent_entry_matrix: bfloat16 [2048, 256], replicated, may hold values from -0.23925781 to 0.23925781
- rare_entry_matrix: float32 [65536, 256], P('shard'), may hold values from -0.24 to 0.24
- frequent_entry_lines: int32 [65536, 4], P(('shard', 'blk')), may hold values from 0 to 2047
- rare_place_parent: int32 [65536, 4], P(('shard', 'blk')), may hold values from 0 to 31, all different within a row; in each aligned block of 256 rows (0 to 255, 256 to 511, ...) at most 64 rows name the same one
- rare_local_position: int32 [65536, 4], P(('shard', 'blk')), may hold values from 0 to 2047
- rare_place_tally: int32 [65536], P(('shard', 'blk')), may hold values from 1 to 4
- sharpness_factor: float32 [1], replicated, may hold values from 4 to 16
- pairscore_additive: float32 [1], replicated, may hold values from -6 to -2
Outputs:
- request_derivative: float32 [65536, 256], P(('shard', 'blk'))
- hot_grad: float32 [2048, 256], replicated
- cold_grad: float32 [65536, 256], P(('shard', 'blk'))
The draws below stay inside these ranges and needn't reach their ends.
Inputs may be any that keep to these rules, and one draw needn't show every extreme that they name: `rare_place_parent`: each row names 4 different owners; among the rows of one device no owner is named by more than 64 rows, a bound that some block reaches.
All inputs are finite; a program needn't handle non-finite values.
Results may differ from the reference program's by a relative error of at most 0.007.
Values may be sent and summed in bfloat16 or wider, within the bound.
No kernel may reach another device: no remote copies, remote signals or barrier semaphores. Data moves between devices by JAX's collectives and lax.ppermute only.
A program may use at most 64 MiB of HBM per device.

```python
import math
import jax
import jax.numpy as jnp
import numpy as np
from jax import lax

E = 256
HB = 4
CB = 4
PAIRS = 256
HOT = 2048
COLD_DEV = 2048
CAP = 64
NP = 65536
COLD_ROWS = 65536
N_SHARD = 32
N_BLK = 8


def place_ends(entries, own_key, low, top_value):
    extent = entries.shape
    place = [jax.random.randint(jax.random.fold_in(own_key, axis), (), 0, extent[axis]) for axis in range(len(extent))]
    entries = entries.at[tuple(place)].set(low)
    longest = extent.index(max(extent))
    place[longest] = (place[longest] + 1) % extent[longest]
    return entries.at[tuple(place)].set(top_value)


def level_of(stream_key, shape, pieces, least, high):
    def one(dim, shards_of):
        draws = jax.random.uniform(jax.random.fold_in(jax.random.fold_in(stream_key, 6), dim), (shards_of,), jnp.float32, least / len(pieces), high / len(pieces))
        return jnp.repeat(jnp.exp(draws), shape[dim] // shards_of).reshape((-1,) + (1,) * (len(shape) - dim - 1))

    gain = one(*pieces[0])
    for cut in pieces[1:]:
        gain = gain * one(*cut)
    return gain


def cumulative_ranks(count, lean):
    portions = [(1 << 20) // math.isqrt(rank ** lean) + 1 for rank in range(1, count + 1)]
    spread = 1 + sum(portions) // (1 << 30)
    return np.cumsum(np.array([max(1, weight // spread) for weight in portions]))


def ranked_ids(own_key, dims, amount, slope):
    table = cumulative_ranks(amount, slope)
    ticket = jax.random.randint(jax.random.fold_in(own_key, 1), dims, 0, int(table[amount - 1]))
    standing = jnp.searchsorted(jnp.asarray(table, jnp.int32), ticket, side="right")
    return jax.random.permutation(jax.random.fold_in(own_key, 2), amount)[standing].astype(jnp.int32)


def routed_block(own_key, own, number, rows, count, top, most, slope):
    ranking = jax.random.permutation(own_key, count)
    packed, common = load_shares(count, rows * top, most, slope, True), load_shares(count, rows * top, most, slope, False)
    places = jnp.arange(count)

    def named(lengths, offset_by):
        used = int((lengths > 0).sum())
        fixed = max(1, used // 4)
        passed = fixed + (places - fixed + offset_by * (used - fixed)) % max(1, count - fixed)
        return jnp.zeros((count,), jnp.int32).at[ranking[jnp.where(places < fixed, places, passed)]].set(jnp.asarray(lengths, jnp.int32))

    lengths = jnp.where(number % 4 == 0, named(packed, number // 4), named(common, number - number // 4 - 1))
    mixed = jax.random.permutation(jax.random.fold_in(own, 3), count)
    giver, receiver = mixed[0:count // 2 * 2:2], mixed[1:count // 2 * 2:2]
    margin = jnp.minimum(lengths[giver] - 1, most - lengths[receiver]) // 2
    margin = jnp.where((giver == ranking[0]) | (receiver == ranking[0]) | (lengths[receiver] == 0), 0, jnp.maximum(margin, 0))
    passed = jax.random.randint(jax.random.fold_in(own, 4), (count // 2,), 0, 1 << 20) % (margin + 1)
    lengths = lengths.at[giver].add(-passed).at[receiver].add(passed)
    members = jnp.searchsorted(jnp.cumsum(lengths), jnp.arange(rows * top), side="right").astype(jnp.int32)
    listing = members.reshape(top, rows).T
    listing = listing[jax.random.permutation(jax.random.fold_in(own, 1), rows)]
    offset_by = jax.random.randint(jax.random.fold_in(own, 2), (rows, 1), 0, top)
    return jnp.take_along_axis(listing, (jnp.arange(top)[None, :] + offset_by) % top, axis=1)


def load_shares(count, total, limit, slope, full):
    portions = [(1 << 20) // math.isqrt(rank ** slope) + 1 for rank in range(1, count + 1)]
    largest = limit if full else min(limit, max(-(-total // count), total * portions[0] // sum(portions)))
    least = 1 if total - largest >= count - 1 else 0
    holding, rest = [largest] + [least] * (count - 1), total - largest - least * (count - 1)
    while rest > 0:
        free = [i for i in range(1, count) if holding[i] < largest] or [i for i in range(1, count) if holding[i] < limit]
        whole, left = sum([portions[i] for i in free]), rest
        for i in free:
            addition = min(limit - holding[i], max(1, left * portions[i] // whole), rest)
            holding[i] = holding[i] + addition
            rest = rest - addition
    return np.array(holding)


def scatter_about(stream_key, dims, deviation, limit, shards=(), held_as=jnp.bfloat16):
    values = jax.random.normal(stream_key, dims, jnp.float32) * deviation
    if len(shards) > 0:
        values = level_of(stream_key, dims, shards, -0.22, 0.18) * values
    return jnp.clip(values, min=-limit, max=limit).astype(held_as)


def setup_inputs(seed: int = 0) -> dict:
    streams_of = jax.random.split(jax.random.key(seed), 10)
    request_embeddings = scatter_about(streams_of[0], (NP, E), 0.0625, 0.5, ((0, 256),))
    frequent_entry_matrix = scatter_about(streams_of[1], (HOT, E), 0.03, 0.23925781)
    rare_entry_matrix = scatter_about(streams_of[2], (COLD_ROWS, E), 0.03, 0.24, ((0, 32),), jnp.float32)
    frequent_entry_lines = place_ends(ranked_ids(streams_of[3], (NP, HB), HOT, 1), jax.random.fold_in(streams_of[3], 3), 0, HOT - 1).astype(jnp.int32)
    rare_place_parent_keys = jax.random.split(jax.random.fold_in(streams_of[4], 1), NP // PAIRS)
    rare_place_parent_turns = jax.random.permutation(jax.random.fold_in(streams_of[4], 3), NP // PAIRS)
    rare_place_parent = jax.vmap(lambda own, number: routed_block(jax.random.fold_in(streams_of[4], 2), own, number, PAIRS, N_SHARD, CB, CAP, 2))(rare_place_parent_keys, rare_place_parent_turns).reshape((NP, CB))
    rare_local_position = place_ends(jax.random.randint(streams_of[5], (NP, CB), 0, COLD_DEV), jax.random.fold_in(streams_of[5], 1), 0, COLD_DEV - 1).astype(jnp.int32)
    rare_place_tally = place_ends(jax.random.randint(streams_of[6], (NP,), 1, CB + 1), jax.random.fold_in(streams_of[6], 1), 1, CB).astype(jnp.int32)
    sharpness_factor = jnp.clip(jnp.exp(jax.random.uniform(streams_of[7], (1,), jnp.float32, math.log(4.0), math.log(16.0))), 4.0, 16.0)
    pairscore_additive = jnp.clip(jax.random.uniform(streams_of[8], (1,), jnp.float32, -6.0, -2.0), -6.0, -2.0)
    return dict(request_embeddings=request_embeddings, frequent_entry_matrix=frequent_entry_matrix, rare_entry_matrix=rare_entry_matrix, frequent_entry_lines=frequent_entry_lines, rare_place_parent=rare_place_parent, rare_local_position=rare_local_position, rare_place_tally=rare_place_tally, sharpness_factor=sharpness_factor, pairscore_additive=pairscore_additive)


epsilon = 1e-06

def normalize_rows(vectors):
    radius = jnp.sqrt(lax.optimization_barrier(jnp.sum(vectors * vectors, axis=1, keepdims=True)) + epsilon)
    return (vectors / radius, radius)

def projection_backward(unit_vectors, radius, gradient):
    inner = lax.optimization_barrier(jnp.sum(unit_vectors * gradient, axis=1, keepdims=True))
    return (gradient - unit_vectors * inner) / radius

def reference(request_embeddings, frequent_entry_matrix, rare_entry_matrix, frequent_entry_lines, rare_place_parent, rare_local_position, rare_place_tally, sharpness_factor, pairscore_additive):
    group_size = PAIRS * N_BLK
    sharpness_multiplier = sharpness_factor[0]
    additive_term = pairscore_additive[0]
    slot_index = jnp.arange(CB, dtype=jnp.int32)
    diagonal = jnp.arange(group_size, dtype=jnp.int32)

    def one_group(running, group_index):
        hot_acc, cold_acc = running
        first_row = (group_index * group_size).astype(jnp.int32)
        features = lax.dynamic_slice_in_dim(request_embeddings, first_row, group_size, 0).astype(jnp.float32)
        hot_slots = lax.dynamic_slice_in_dim(frequent_entry_lines, first_row, group_size, 0)
        owners = lax.dynamic_slice_in_dim(rare_place_parent, first_row, group_size, 0)
        offsets = lax.dynamic_slice_in_dim(rare_local_position, first_row, group_size, 0)
        counts = lax.dynamic_slice_in_dim(rare_place_tally, first_row, group_size, 0)
        cold_rows = (owners * COLD_DEV + offsets).astype(jnp.int32)
        live_slot = (slot_index[None, :] < counts[:, None]).astype(jnp.float32)
        hot_sum = lax.optimization_barrier(jnp.sum(jnp.take(frequent_entry_matrix, hot_slots, axis=0).astype(jnp.float32), axis=1))
        cold_sum = lax.optimization_barrier(jnp.sum(jnp.take(rare_entry_matrix, cold_rows, axis=0) * live_slot[:, :, None], axis=1))
        candidate_normalized, candidate_norm = normalize_rows(hot_sum + cold_sum)
        request_normalized, request_norm = normalize_rows(features)
        candidate_reduced = candidate_normalized.astype(jnp.bfloat16)
        request_reduced = request_normalized.astype(jnp.bfloat16)
        pairwise_scores = sharpness_multiplier * lax.dot_general(request_reduced, candidate_reduced, (((1,), (1,)), ((), ())), preferred_element_type=jnp.float32) + additive_term
        positive = (diagonal[:, None] == diagonal[None, :]).astype(jnp.float32)
        pairscore_derivative = (jax.nn.sigmoid(pairwise_scores) - positive).astype(jnp.bfloat16)
        request_direction = sharpness_multiplier * jnp.dot(pairscore_derivative, candidate_reduced, preferred_element_type=jnp.float32)
        candidate_direction = sharpness_multiplier * lax.dot_general(pairscore_derivative, request_reduced, (((0,), (0,)), ((), ())), preferred_element_type=jnp.float32)
        request_derivative = projection_backward(request_normalized, request_norm, request_direction)
        item_low_grad = lax.optimization_barrier(projection_backward(candidate_normalized, candidate_norm, candidate_direction).astype(jnp.bfloat16))
        candidate_derivative = item_low_grad.astype(jnp.float32)
        hot_acc = hot_acc.at[hot_slots.reshape(-1)].add(jnp.repeat(candidate_derivative, HB, axis=0))
        cold_terms = jnp.repeat(candidate_derivative, CB, axis=0) * live_slot.reshape(-1)[:, None]
        cold_acc = cold_acc.at[cold_rows.reshape(-1)].add(cold_terms)
        return ((hot_acc, cold_acc), request_derivative)
    start_state = (jnp.zeros((HOT, E), jnp.float32), jnp.zeros((N_SHARD * COLD_DEV, E), jnp.float32))
    (hot_grad, cold_grad), query_parts = lax.scan(one_group, start_state, jnp.arange(N_SHARD, dtype=jnp.int32))
    return (query_parts.reshape(N_SHARD * group_size, E), hot_grad, cold_grad)
```

```python
import jax
import jax.numpy as jnp
from jax import lax
from jax.experimental import pallas as pl
from jax.experimental.pallas import tpu as pltpu
from jax.sharding import PartitionSpec as P

epsilon = 1e-06
F32 = jnp.float32
BF16 = jnp.bfloat16
NN = (((1,), (0,)), ((), ()))
NT = (((1,), (1,)), ((), ()))


def mm(a, b, dims=NN):
    return lax.dot_general(a, b, dims, preferred_element_type=F32)


def iota(shape, dim):
    return lax.broadcasted_iota(jnp.int32, shape, dim)


def call(kernel, outs, *args, smem=0, scratch=(), flops=0, grid=None, in_specs=None, out_specs=None):
    moved = sum(a.size * a.dtype.itemsize for a in args) + sum(o.size * o.dtype.itemsize for o in outs)
    extra = {}
    if grid is not None:
        extra = dict(grid=grid, in_specs=in_specs, out_specs=out_specs)
    else:
        spaces = [pltpu.SMEM] * smem + [pltpu.VMEM] * (len(args) - smem)
        extra = dict(
            in_specs=[pl.BlockSpec(memory_space=s) for s in spaces],
            out_specs=[pl.BlockSpec(memory_space=pltpu.VMEM) for _ in outs],
        )
    return pl.pallas_call(
        kernel,
        out_shape=list(outs),
        scratch_shapes=list(scratch),
        cost_estimate=pl.CostEstimate(flops=flops, bytes_accessed=moved, transcendentals=0),
        **extra,
    )(*args)


def shape(dims, dtype):
    return jax.ShapeDtypeStruct(dims, dtype)


def expander(owners, cap, base, width):
    return ((iota((owners, width), 1) + base) // cap == iota((owners, width), 0)).astype(F32).astype(BF16)


def make_requests(owners, cap):
    def kernel(parent_ref, place_ref, tally_ref, rank_ref, ask_ref, row_ref):
        pairs, slots = parent_ref.shape
        lane = iota((pairs, owners), 1)
        tally = tally_ref[...]
        named = jnp.zeros((pairs, owners), F32)
        high = jnp.zeros((pairs, owners), F32)
        low = jnp.zeros((pairs, owners), F32)
        for c in range(slots):
            hit = jnp.logical_and(parent_ref[:, c : c + 1] == lane, tally > c)
            place = place_ref[:, c : c + 1]
            named = jnp.where(hit, 1.0, named)
            high = jnp.where(hit, (place // 64).astype(F32), high)
            low = jnp.where(hit, (place % 64).astype(F32), low)
        before = (iota((pairs, pairs), 0) > iota((pairs, pairs), 1)).astype(F32).astype(BF16)
        rank = jnp.where(named > 0, mm(before, named.astype(BF16)), -1.0)
        rank_ref[...] = rank
        rank, high, low = rank.astype(BF16), high.astype(BF16), low.astype(BF16)
        total = owners * cap
        width = 512
        for base in range(0, total, width):
            spread = expander(owners, cap, base, width)
            want = (iota((pairs, width), 1) % cap).astype(F32)
            place = mm(high, spread) * 64.0 + mm(low, spread)
            row_ref[:, base : base + width] = jnp.sum(
                jnp.where(mm(rank, spread) == want, place, 0.0), axis=0, keepdims=True
            )
        for o in range(owners):
            ask_ref[o : o + 1, :] = row_ref[:, o * cap : (o + 1) * cap].astype(jnp.int32)

    return kernel


def prepare(owners, cap):
    def kernel(rank_ref, rank_t_ref, lines_ref, hot_ref, query_ref,
               pick_ref, place_ref, hot_sum_ref, unit_ref, radius_ref, low_ref):
        pairs = rank_ref.shape[0]
        total = owners * cap
        width = 256
        rank = rank_ref[...].astype(BF16)
        rank_t = rank_t_ref[...].astype(BF16)
        hot_sum_ref[...] = jnp.zeros_like(hot_sum_ref)

        def step(i, _):
            base = pl.multiple_of(i * width, width)
            spread = expander(owners, cap, base, width)
            want = (iota((pairs, width), 1) % cap).astype(F32)
            pick_ref[:, pl.ds(base, width)] = (mm(rank, spread) == want).astype(F32).astype(BF16)
            spread_t = ((iota((width, owners), 0) + base) // cap == iota((width, owners), 1))
            want_t = (iota((width, pairs), 0) % cap).astype(F32)
            hit = mm(spread_t.astype(F32).astype(BF16), rank_t) == want_t
            place_ref[pl.ds(base, width), :] = hit.astype(F32).astype(BF16)
            column = iota((pairs, width), 1) + base
            counts = jnp.zeros((pairs, width), F32)
            for h in range(lines_ref.shape[1]):
                counts += (lines_ref[:, h : h + 1] == column).astype(F32)
            hot_sum_ref[...] += mm(counts.astype(BF16), hot_ref[pl.ds(base, width), :])
            return 0

        lax.fori_loop(0, total // width, step, 0)
        query = query_ref[...].astype(F32)
        radius = jnp.sqrt(jnp.sum(query * query, axis=1, keepdims=True) + epsilon)
        unit = query / radius
        unit_ref[...] = unit
        radius_ref[...] = radius
        low_ref[...] = unit.astype(BF16)

    return kernel


def fetch(ask_ref, table_ref, out_ref, low_ref):
    rows = table_ref.shape[0]
    width = ask_ref.shape[1]

    @pl.when(pl.program_id(0) == 0)
    def _():
        low_ref[...] = table_ref[...].astype(BF16)

    ask = ask_ref[pl.ds(pl.program_id(0), 1), :]
    diagonal = iota((width, width), 0) == iota((width, width), 1)
    column = jnp.sum(jnp.where(diagonal, ask, 0).astype(F32), axis=1, keepdims=True).astype(jnp.int32)
    hit = (column == iota((width, rows), 1)).astype(F32).astype(BF16)
    out_ref[...] = mm(hit, low_ref[...]).astype(BF16)


def loss_side(own_low, others_ref, total_ref, own_block, sharpness, additive):
    rows = own_low.shape[0]
    width = 256
    total_ref[...] = jnp.zeros_like(total_ref)

    def step(i, _):
        base = pl.multiple_of(i * width, width)
        other = others_ref[pl.ds(base, width), :]
        logits = sharpness * mm(own_low, other, NT) + additive
        same = iota((rows, width), 0) + own_block * rows == iota((rows, width), 1) + base
        grad = (jax.nn.sigmoid(logits) - same.astype(F32)).astype(BF16)
        total_ref[...] += mm(grad, other)
        return 0

    lax.fori_loop(0, others_ref.shape[0] // width, step, 0)
    return sharpness * total_ref[...]


def project(unit, radius, direction):
    inner = jnp.sum(unit * direction, axis=1, keepdims=True)
    return (direction - unit * inner) / radius


def item_side(block_ref, sharp_ref, add_ref, fetched_ref, pick_ref, place_ref, hot_sum_ref, queries_ref,
              low_ref, grad_ref, out_ref, total_ref):
    item = hot_sum_ref[...] + mm(pick_ref[...], fetched_ref[...])
    radius = jnp.sqrt(jnp.sum(item * item, axis=1, keepdims=True) + epsilon)
    unit = item / radius
    low = unit.astype(BF16)
    low_ref[...] = low
    direction = loss_side(low, queries_ref, total_ref, block_ref[0], sharp_ref[0], add_ref[0])
    grad = project(unit, radius, direction).astype(BF16)
    grad_ref[...] = grad
    width = 256

    def step(i, _):
        base = pl.multiple_of(i * width, width)
        out_ref[pl.ds(base, width), :] = mm(place_ref[pl.ds(base, width), :], grad).astype(BF16)
        return 0

    lax.fori_loop(0, out_ref.shape[0] // width, step, 0)


def query_side(block_ref, sharp_ref, add_ref, unit_ref, radius_ref, items_ref, out_ref, total_ref):
    unit = unit_ref[...]
    direction = loss_side(unit.astype(BF16), items_ref, total_ref, block_ref[0], sharp_ref[0], add_ref[0])
    out_ref[...] = project(unit, radius_ref[...], direction)


def hot_terms(lines_t_ref, grad_ref, out_ref):
    width, pairs = out_ref.shape[0], grad_ref.shape[0]
    row = iota((width, pairs), 0) + pl.program_id(0) * width
    counts = jnp.zeros((width, pairs), F32)
    for h in range(lines_t_ref.shape[0]):
        counts += (lines_t_ref[h : h + 1, :] == row).astype(F32)
    out_ref[...] = mm(counts.astype(BF16), grad_ref[...]).astype(BF16)


def cold_terms(ask_ref, grad_ref, out_ref):
    width, total = out_ref.shape[0], grad_ref.shape[0]
    row = iota((width, total), 0) + pl.program_id(0) * width
    hit = (ask_ref[...] == row).astype(F32).astype(BF16)
    out_ref[...] = mm(hit, grad_ref[...]).astype(BF16)


def whole(array):
    return pl.BlockSpec(array.shape, lambda i: (0,) * array.ndim)


def swap(array, axis):
    return lax.all_to_all(array, axis, split_axis=0, concat_axis=0, tiled=True)


def spread(array, axis):
    return swap(jnp.broadcast_to(array[None], (lax.axis_size(axis),) + array.shape), axis)


def body(queries, hot_table, cold_table, lines, parent, place, tally, sharpness, additive):
    pairs, width = queries.shape
    owners, blocks = lax.axis_size("shard"), lax.axis_size("blk")
    slots = parent.shape[1]
    cap = 2 * pairs * slots // owners
    total = owners * cap
    rows = cold_table.shape[0]
    hot_rows = hot_table.shape[0]
    block = lax.axis_index("blk").astype(jnp.int32).reshape(1)
    step = 256

    rank, ask = call(
        make_requests(owners, cap),
        [shape((pairs, owners), F32), shape((owners, cap), jnp.int32)],
        parent, place, tally.reshape(pairs, 1),
        scratch=[pltpu.VMEM((1, total), F32)],
        flops=2 * pairs * total * owners * 3,
    )
    asked = swap(ask.reshape(owners, 1, cap), "shard").reshape(total // step, step)

    pick, placed, hot_sum, unit, radius, query_low = call(
        prepare(owners, cap),
        [
            shape((pairs, total), BF16),
            shape((total, pairs), BF16),
            shape((pairs, width), F32),
            shape((pairs, width), F32),
            shape((pairs, 1), F32),
            shape((pairs, width), BF16),
        ],
        rank, rank.T, lines, hot_table, queries,
        flops=2 * pairs * total * (width + 2 * owners),
    )
    all_queries = spread(query_low, "blk").reshape(blocks * pairs, width)

    (looked,) = call(
        fetch,
        [shape((total, width), BF16)],
        asked, cold_table,
        grid=(total // step,),
        in_specs=[whole(asked), whole(cold_table)],
        out_specs=[pl.BlockSpec((step, width), lambda i: (i, 0))],
        scratch=[pltpu.VMEM((rows, width), BF16)],
        flops=2 * total * rows * width,
    )
    fetched = swap(looked.reshape(owners, cap, width), "shard").reshape(total, width)

    item_low, item_grad, outgoing = call(
        item_side,
        [shape((pairs, width), BF16), shape((pairs, width), BF16), shape((total, width), BF16)],
        block, sharpness, additive, fetched, pick, placed, hot_sum, all_queries,
        smem=3,
        scratch=[pltpu.VMEM((pairs, width), F32)],
        flops=2 * pairs * width * (2 * total + 2 * blocks * pairs),
    )
    incoming = swap(outgoing.reshape(owners, cap, width), "shard").reshape(total, width)

    (hot_local,) = call(
        hot_terms,
        [shape((hot_rows, width), BF16)],
        lines.T, item_grad,
        grid=(hot_rows // step,),
        in_specs=[pl.BlockSpec((slots, pairs), lambda i: (0, 0)), whole(item_grad)],
        out_specs=[pl.BlockSpec((step, width), lambda i: (i, 0))],
        flops=2 * pairs * hot_rows * width,
    )
    hot_parts = swap(hot_local.reshape(blocks, hot_rows // blocks, width), "blk")
    hot_block = jnp.sum(hot_parts.astype(F32), axis=0).astype(BF16)
    hot_parts = swap(hot_block.reshape(owners, hot_rows // blocks // owners, width), "shard")
    hot_piece = jnp.sum(hot_parts.astype(F32), axis=0).astype(BF16)
    hot_block = spread(hot_piece, "shard").reshape(hot_rows // blocks, width)
    hot_grad = spread(hot_block, "blk").reshape(hot_rows, width).astype(F32)

    all_items = spread(item_low, "blk").reshape(blocks * pairs, width)
    (query_grad,) = call(
        query_side,
        [shape((pairs, width), F32)],
        block, sharpness, additive, unit, radius, all_items,
        smem=3,
        scratch=[pltpu.VMEM((pairs, width), F32)],
        flops=4 * pairs * width * blocks * pairs,
    )

    (cold_local,) = call(
        cold_terms,
        [shape((rows, width), BF16)],
        asked.reshape(1, total), incoming,
        grid=(rows // step,),
        in_specs=[pl.BlockSpec((1, total), lambda i: (0, 0)), whole(incoming)],
        out_specs=[pl.BlockSpec((step, width), lambda i: (i, 0))],
        flops=2 * total * rows * width,
    )
    cold_parts = swap(cold_local.reshape(blocks, rows // blocks, width), "blk")
    cold_grad = jnp.sum(cold_parts.astype(F32), axis=0)
    return (query_grad, hot_grad, cold_grad)


def solution(mesh):
    pair = P(("shard", "blk"), None)
    in_specs = (pair, P(), P("shard", None), pair, pair, pair, P(("shard", "blk")), P(), P())
    return jax.shard_map(body, mesh=mesh, in_specs=in_specs, out_specs=(pair, P(), pair), check_vma=False)
```

```python
import jax
import jax.numpy as jnp
from jax import lax
from jax.experimental import pallas as pl
from jax.experimental.pallas import tpu as pltpu
from jax.sharding import PartitionSpec as P

epsilon = 1e-06
F32 = jnp.float32
BF16 = jnp.bfloat16
NN = (((1,), (0,)), ((), ()))
NT = (((1,), (1,)), ((), ()))


def mm(a, b, dims=NN):
    return lax.dot_general(a, b, dims, preferred_element_type=F32)


def iota(shape, dim):
    return lax.broadcasted_iota(jnp.int32, shape, dim)


def call(kernel, outs, *args, smem=0, scratch=(), flops=0, grid=None, in_specs=None, out_specs=None):
    moved = sum(a.size * a.dtype.itemsize for a in args) + sum(o.size * o.dtype.itemsize for o in outs)
    extra = {}
    if grid is not None:
        extra = dict(grid=grid, in_specs=in_specs, out_specs=out_specs)
    else:
        spaces = [pltpu.SMEM] * smem + [pltpu.VMEM] * (len(args) - smem)
        extra = dict(
            in_specs=[pl.BlockSpec(memory_space=s) for s in spaces],
            out_specs=[pl.BlockSpec(memory_space=pltpu.VMEM) for _ in outs],
        )
    return pl.pallas_call(
        kernel,
        out_shape=list(outs),
        scratch_shapes=list(scratch),
        compiler_params=pltpu.CompilerParams(vmem_limit_bytes=24 << 20),
        cost_estimate=pl.CostEstimate(flops=flops, bytes_accessed=moved, transcendentals=0),
        **extra,
    )(*args)


def shape(dims, dtype):
    return jax.ShapeDtypeStruct(dims, dtype)


def expander(owners, cap, base, width):
    return ((iota((owners, width), 1) + base) // cap == iota((owners, width), 0)).astype(F32).astype(BF16)


LANES = 128


def make_requests(owners, cap):
    def kernel(parent_ref, place_ref, tally_ref, rank_ref, rank_t_ref, ask_ref, row_ref):
        slots, pairs = parent_ref.shape
        line = iota((LANES, pairs), 0)
        tally = tally_ref[...]
        named = jnp.zeros((LANES, pairs), F32)
        where = jnp.zeros((LANES, pairs), F32)
        for c in range(slots):
            hit = jnp.logical_and(parent_ref[c : c + 1, :] == line, tally > c)
            named = jnp.where(hit, 1.0, named)
            where = jnp.where(hit, place_ref[c : c + 1, :].astype(F32), where)
        before = (iota((pairs, pairs), 0) < iota((pairs, pairs), 1)).astype(F32).astype(BF16)
        rank_t = jnp.where(named > 0, mm(named.astype(BF16), before), -1.0)
        rank = rank_t.T
        rank_t_ref[...] = rank_t.astype(BF16)
        rank_ref[...] = rank.astype(BF16)
        where = where.T.astype(jnp.int32)
        high = (where // 64).astype(F32).astype(BF16)
        low = (where % 64).astype(F32).astype(BF16)
        rank = rank.astype(BF16)
        total = owners * cap
        width = 512
        for base in range(0, total, width):
            spread = expander(LANES, cap, base, width)
            want = (iota((pairs, width), 1) % cap).astype(F32)
            place = mm(high, spread) * 64.0 + mm(low, spread)
            row_ref[:, base : base + width] = jnp.sum(
                jnp.where(mm(rank, spread) == want, place, 0.0), axis=0, keepdims=True
            )
        for o in range(owners):
            ask = row_ref[:, o * cap : (o + 1) * cap].astype(jnp.int32)
            ask_ref[o, :, 0:cap] = jnp.broadcast_to(ask, (ask_ref.shape[1], cap))

    return kernel


def unit_queries(query_ref, lines_ref, unit_ref, radius_ref, send_ref):
    pairs = query_ref.shape[0]
    slots = lines_ref.shape[0]
    query = query_ref[...].astype(F32)
    radius = jnp.sqrt(jnp.sum(query * query, axis=1, keepdims=True) + epsilon)
    unit = query / radius
    unit_ref[...] = unit
    radius_ref[...] = radius
    send_ref[0:pairs, :] = unit.astype(BF16)
    tail = send_ref.shape[0] - pairs
    line = iota((tail, pairs), 0)
    extra = jnp.zeros((tail, pairs), F32)
    for h in range(slots):
        row = lines_ref[h : h + 1, :]
        extra = jnp.where(line == h, (row // 64).astype(F32), extra)
        extra = jnp.where(line == h + slots, (row % 64).astype(F32), extra)
    send_ref[pairs:, :] = extra.astype(BF16)


def prepare(owners, cap):
    def kernel(rank_ref, rank_t_ref, lines_ref, hot_ref, table_ref, table_low_ref,
               pick_ref, place_ref, hot_sum_ref):
        pairs = rank_ref.shape[0]
        slots = lines_ref.shape[0]
        total = owners * cap
        width = 256
        rank = rank_ref[...]
        rank_t = rank_t_ref[...]
        hot_sum_ref[...] = jnp.zeros_like(hot_sum_ref)
        line = iota((LANES, pairs), 0)
        lines = jnp.zeros((LANES, pairs), F32)
        for h in range(slots):
            lines = jnp.where(line == h, lines_ref[h : h + 1, :].astype(F32), lines)
        lines = lines.T.astype(jnp.int32)

        def step(i, _):
            base = pl.multiple_of(i * width, width)
            table_low_ref[pl.ds(base, width), :] = table_ref[pl.ds(base, width), :].astype(BF16)
            spread = expander(LANES, cap, base, width)
            want = (iota((pairs, width), 1) % cap).astype(F32)
            pick_ref[:, pl.ds(base, width)] = (mm(rank, spread) == want).astype(F32).astype(BF16)
            spread_t = ((iota((width, LANES), 0) + base) // cap == iota((width, LANES), 1))
            want_t = (iota((width, pairs), 0) % cap).astype(F32)
            hit = mm(spread_t.astype(F32).astype(BF16), rank_t) == want_t
            place_ref[pl.ds(base, width), :] = hit.astype(F32).astype(BF16)
            column = iota((pairs, width), 1) + base
            counts = jnp.zeros((pairs, width), F32)
            for h in range(slots):
                counts += (lines[:, h : h + 1] == column).astype(F32)
            hot_sum_ref[...] += mm(counts.astype(BF16), hot_ref[pl.ds(base, width), :])
            return 0

        lax.fori_loop(0, total // width, step, 0)

    return kernel


def fetch(ask_ref, table_ref, out_ref):
    rows = table_ref.shape[0]
    group, cap = out_ref.shape[0], out_ref.shape[1]
    diagonal = iota((cap, cap), 0) == iota((cap, cap), 1)
    columns = []
    for g in range(group):
        ask = ask_ref[pl.program_id(0) * group + g, 0:1, 0:cap]
        columns.append(jnp.sum(jnp.where(diagonal, ask, 0).astype(F32), axis=1, keepdims=True))
    column = jnp.concatenate(columns, axis=0).astype(jnp.int32)
    hit = (column == iota((group * cap, rows), 1)).astype(F32).astype(BF16)
    out_ref[...] = mm(hit, table_ref[...]).astype(BF16).reshape(out_ref.shape)


def loss_side(own_low, other_refs, total_ref, sharpness, additive):
    rows = own_low.shape[0]
    for i, ref in enumerate(other_refs):
        other = ref[0:rows, :]
        grad = jax.nn.sigmoid(sharpness * mm(own_low, other, NT) + additive)
        if i == 0:
            grad = grad - (iota((rows, rows), 0) == iota((rows, rows), 1)).astype(F32)
            total_ref[...] = mm(grad.astype(BF16), other)
        else:
            total_ref[...] += mm(grad.astype(BF16), other)
    return sharpness * total_ref[...]


def project(unit, radius, direction):
    inner = jnp.sum(unit * direction, axis=1, keepdims=True)
    return (direction - unit * inner) / radius


def item_side(blocks):
    def kernel(sharp_ref, add_ref, fetched_ref, pick_ref, place_ref, hot_sum_ref, *refs):
        query_refs, (low_ref, grad_ref, out_ref, total_ref) = refs[:blocks], refs[blocks:]
        item = hot_sum_ref[...] + mm(pick_ref[...], fetched_ref[...])
        radius = jnp.sqrt(jnp.sum(item * item, axis=1, keepdims=True) + epsilon)
        unit = item / radius
        low = unit.astype(BF16)
        low_ref[...] = low
        direction = loss_side(low, query_refs, total_ref, sharp_ref[0], add_ref[0])
        grad = project(unit, radius, direction).astype(BF16)
        grad_ref[...] = grad
        width = 256

        def step(i, _):
            base = pl.multiple_of(i * width, width)
            out_ref[pl.ds(base, width), :] = mm(place_ref[pl.ds(base, width), :], grad).astype(BF16)
            return 0

        lax.fori_loop(0, out_ref.shape[0] // width, step, 0)

    return kernel


def query_side(sharp_ref, add_ref, unit_ref, radius_ref, *refs):
    item_refs, (out_ref, total_ref) = refs[:-2], refs[-2:]
    unit = unit_ref[...]
    direction = loss_side(unit.astype(BF16), item_refs, total_ref, sharp_ref[0], add_ref[0])
    out_ref[...] = project(unit, radius_ref[...], direction)


def hot_terms(blocks, slots):
    def kernel(block_ref, *refs):
        grad_refs, line_refs, (out_ref, total_ref) = refs[:blocks], refs[blocks : 2 * blocks], refs[2 * blocks :]
        width, pairs = out_ref.shape[0], grad_refs[0].shape[0]
        row = (iota((width, pairs), 0) + block_ref[0] * width).astype(F32)
        total_ref[...] = jnp.zeros_like(total_ref)
        for grad_ref, line_ref in zip(grad_refs, line_refs):
            lines = line_ref[pairs:, :].astype(F32)
            counts = jnp.zeros((width, pairs), F32)
            for h in range(slots):
                counts += (lines[h : h + 1, :] * 64.0 + lines[h + slots : h + slots + 1, :] == row).astype(F32)
            total_ref[...] += mm(counts.astype(BF16), grad_ref[...])
        out_ref[...] = total_ref[...].astype(BF16)

    return kernel


def hot_sum_spread(parts_ref, out_ref):
    piece = jnp.sum(parts_ref[...].astype(F32), axis=0, keepdims=True)
    out_ref[...] = jnp.broadcast_to(piece, out_ref.shape).astype(BF16)


def widen(blocks):
    def kernel(block_ref, *refs):
        part_refs, out_ref = refs[:blocks], refs[blocks]
        chips = blocks // 2
        width = part_refs[0].shape[0]
        mine, core = block_ref[0] // 2, block_ref[0] % 2
        for i, ref in enumerate(part_refs):
            chip = (mine + chips - i % chips) % chips
            index = chip * 2 + (core if i < chips else 1 - core)
            out_ref[pl.ds(pl.multiple_of(index * width, width), width), :] = ref[...].astype(F32)

    return kernel


def cold_terms(same_core):
    def kernel(block_ref, ask_ref, grad_ref, out_ref, row_ref):
        width, total = out_ref.shape[1], grad_ref.shape[0]
        owners, chips = ask_ref.shape[0], pl.num_programs(0)
        cap = total // owners

        @pl.when(pl.program_id(0) == 0)
        def _():
            for o in range(owners):
                row_ref[:, o * cap : (o + 1) * cap] = ask_ref[o, 0:1, 0:cap]

        core = block_ref[0] % 2
        core = core if same_core else 1 - core
        chip = (block_ref[0] // 2 + pl.program_id(0)) % chips
        row = iota((width, total), 0) + (chip * 2 + core) * width
        hit = (row_ref[...] == row).astype(F32).astype(BF16)
        out_ref[0] = mm(hit, grad_ref[...]).astype(out_ref.dtype)

    return kernel


def cold_join(mine_ref, theirs_ref, keep_ref, *send_refs):
    keep_ref[...] = mine_ref[0] + theirs_ref[0].astype(F32)
    for d, ref in enumerate(send_refs):
        ref[...] = (mine_ref[d + 1] + theirs_ref[d + 1].astype(F32)).astype(BF16)


def add_parts(keep_ref, *refs):
    part_refs, out_ref = refs[:-1], refs[-1]
    total = keep_ref[...]
    for ref in part_refs:
        total += ref[...].astype(F32)
    out_ref[...] = total


def whole(array):
    return pl.BlockSpec(array.shape, lambda i: (0,) * array.ndim)


def swap(array, axis):
    return lax.all_to_all(array, axis, split_axis=0, concat_axis=0, tiled=True)


def cross(array, blocks):
    return lax.ppermute(array, "blk", [(i, i ^ 1) for i in range(blocks)])


def shift(array, blocks, d):
    return lax.ppermute(array, "blk", [(i, (i + 2 * d) % blocks) for i in range(blocks)])


def gather_blocks(array, blocks):
    first = cross(array, blocks)
    mine = [shift(array, blocks, d) for d in range(1, blocks // 2)]
    return [array] + mine + [first] + [cross(m, blocks) for m in mine]


def body(queries, hot_table, cold_table, lines, parent, place, tally, sharpness, additive):
    pairs, width = queries.shape
    owners, blocks = lax.axis_size("shard"), lax.axis_size("blk")
    chips = blocks // 2
    slots = parent.shape[1]
    cap = 2 * pairs * slots // owners
    total = owners * cap
    rows = cold_table.shape[0]
    hot_rows = hot_table.shape[0]
    block = lax.axis_index("blk").astype(jnp.int32).reshape(1)

    rank, rank_t, ask = call(
        make_requests(owners, cap),
        [shape((pairs, LANES), BF16), shape((LANES, pairs), BF16), shape((owners, 8, LANES), jnp.int32)],
        parent.T, place.T, tally.reshape(1, pairs),
        scratch=[pltpu.VMEM((1, total), F32)],
        flops=2 * pairs * total * LANES * 3,
    )
    with jax.named_scope("ask"):
        asked = swap(ask, "shard")

    unit, radius, query_block = call(
        unit_queries,
        [shape((pairs, width), F32), shape((pairs, 1), F32), shape((pairs + 16, width), BF16)],
        queries, lines.T,
    )
    with jax.named_scope("queries"):
        query_blocks = gather_blocks(query_block, blocks)

    table_low, pick, placed, hot_sum = call(
        prepare(owners, cap),
        [
            shape((rows, width), BF16),
            shape((pairs, total), BF16),
            shape((total, pairs), BF16),
            shape((pairs, width), F32),
        ],
        rank, rank_t, lines.T, hot_table, cold_table,
        flops=2 * pairs * total * (width + 2 * LANES),
    )

    group = 4
    (looked,) = call(
        fetch,
        [shape((owners, cap, width), BF16)],
        asked, table_low,
        grid=(owners // group,),
        in_specs=[whole(asked), whole(table_low)],
        out_specs=[pl.BlockSpec((group, cap, width), lambda i: (i, 0, 0))],
        flops=2 * total * rows * width,
    )
    with jax.named_scope("rows"):
        fetched = swap(looked, "shard").reshape(total, width)

    item_low, item_grad, outgoing = call(
        item_side(blocks),
        [shape((pairs, width), BF16), shape((pairs, width), BF16), shape((total, width), BF16)],
        sharpness, additive, fetched, pick, placed, hot_sum, *query_blocks,
        smem=2,
        scratch=[pltpu.VMEM((pairs, width), F32)],
        flops=2 * pairs * width * (2 * total + 2 * blocks * pairs),
    )
    with jax.named_scope("cold"):
        incoming = swap(outgoing.reshape(owners, cap, width), "shard").reshape(total, width)

    with jax.named_scope("grads"):
        grad_blocks = gather_blocks(item_grad, blocks)
    (hot_block,) = call(
        hot_terms(blocks, slots),
        [shape((hot_rows // blocks, width), BF16)],
        block, *grad_blocks, *query_blocks,
        smem=1,
        scratch=[pltpu.VMEM((hot_rows // blocks, width), F32)],
        flops=2 * blocks * pairs * width * hot_rows // blocks,
    )
    with jax.named_scope("hot_parts"):
        hot_parts = swap(hot_block.reshape(owners, hot_rows // blocks // owners, width), "shard")
    (hot_piece,) = call(hot_sum_spread, [shape(hot_parts.shape, BF16)], hot_parts)
    with jax.named_scope("hot_whole"):
        hot_block = swap(hot_piece, "shard").reshape(hot_rows // blocks, width)
    with jax.named_scope("hot_blocks"):
        hot_blocks = gather_blocks(hot_block, blocks)
    (hot_grad,) = call(widen(blocks), [shape((hot_rows, width), F32)], block, *hot_blocks, smem=1)

    with jax.named_scope("items"):
        item_blocks = gather_blocks(item_low, blocks)
    (query_grad,) = call(
        query_side,
        [shape((pairs, width), F32)],
        sharpness, additive, unit, radius, *item_blocks,
        smem=2,
        scratch=[pltpu.VMEM((pairs, width), F32)],
        flops=4 * pairs * width * blocks * pairs,
    )

    def cold_half(same_core, dtype):
        return call(
            cold_terms(same_core),
            [shape((chips, rows // blocks, width), dtype)],
            block, asked, incoming,
            grid=(chips,),
            in_specs=[pl.BlockSpec(memory_space=pltpu.SMEM), whole(asked), whole(incoming)],
            out_specs=[pl.BlockSpec((1, rows // blocks, width), lambda i: (i, 0, 0))],
            scratch=[pltpu.VMEM((1, total), jnp.int32)],
            flops=total * rows * width,
        )[0]

    theirs = cold_half(False, BF16)
    with jax.named_scope("cold_cross"):
        theirs = cross(theirs, blocks)
    mine = cold_half(True, F32)
    keep, *sends = call(
        cold_join,
        [shape((rows // blocks, width), F32)] + [shape((rows // blocks, width), BF16)] * (chips - 1),
        mine, theirs,
    )
    with jax.named_scope("cold_shift"):
        parts = [shift(part, blocks, d + 1) for d, part in enumerate(sends)]
    (cold_grad,) = call(add_parts, [shape((rows // blocks, width), F32)], keep, *parts)
    return (query_grad, hot_grad, cold_grad)


def solution(mesh):
    pair = P(("shard", "blk"), None)
    in_specs = (pair, P(), P("shard", None), pair, pair, pair, P(("shard", "blk")), P(), P())
    return jax.shard_map(body, mesh=mesh, in_specs=in_specs, out_specs=(pair, P(), pair), check_vma=False)
```

```python
import jax
import jax.numpy as jnp
from jax import lax
from jax.experimental import pallas as pl
from jax.experimental.pallas import tpu as pltpu
from jax.sharding import PartitionSpec as P


epsilon = 1e-06
F32 = jnp.float32
BF16 = jnp.bfloat16
NN = (((1,), (0,)), ((), ()))
NT = (((1,), (1,)), ((), ()))


def mm(a, b, dims=NN):
    return lax.dot_general(a, b, dims, preferred_element_type=F32)


def iota(shape, dim):
    return lax.broadcasted_iota(jnp.int32, shape, dim)


HBM = pltpu.HBM


class Late:
    def __init__(self, source, buffer, sem):
        self.copy = pltpu.make_async_copy(source, buffer, sem)
        self.buffer = buffer
        self.copy.start()
        self.waits = True

    def get(self):
        if self.waits:
            self.copy.wait()
            self.waits = False
        return self.buffer


def call(kernel, outs, *args, kinds=None, scratch=(), flops=0, grid=(1,), in_specs=None, out_specs=None):
    kinds = kinds or ["v"] * len(args)
    late = [k for k, kind in enumerate(kinds) if isinstance(kind, slice)]
    specs, operands = [], []
    for k, (kind, arg) in enumerate(zip(kinds, args)):
        if kind == "s":
            specs.append(pl.BlockSpec(memory_space=pltpu.SMEM))
        elif k in late:
            specs.append(pl.BlockSpec(memory_space=HBM))
            arg = pltpu.with_memory_space_constraint(arg, HBM)
        else:
            specs.append(in_specs[k] if in_specs else whole(arg))
            if kind == "h":
                arg = pltpu.with_memory_space_constraint(arg, HBM)
        operands.append(arg)
    buffers = []
    for k in late:
        rows = kinds[k].stop - kinds[k].start
        buffers.append(pltpu.VMEM((rows,) + args[k].shape[1:], args[k].dtype))

    def run(*refs):
        refs, extra = list(refs[: len(refs) - len(late) - 1]), refs[len(refs) - len(late) - 1 :]
        for n, k in enumerate(late):
            refs[k] = Late(refs[k].at[kinds[k]], extra[n], extra[-1].at[n])
        kernel(*refs)

    moved = sum(a.size * a.dtype.itemsize for a in args)
    return pl.pallas_call(
        run if late else kernel,
        out_shape=list(outs),
        grid=grid,
        in_specs=specs,
        out_specs=out_specs or [whole(o) for o in outs],
        scratch_shapes=list(scratch) + (buffers + [pltpu.SemaphoreType.DMA((len(late),))] if late else []),
        compiler_params=pltpu.CompilerParams(vmem_limit_bytes=24 << 20),
        cost_estimate=pl.CostEstimate(flops=flops, bytes_accessed=moved, transcendentals=0),
    )(*operands)


def shape(dims, dtype):
    return jax.ShapeDtypeStruct(dims, dtype)


def expander(owners, cap, base, width):
    return ((iota((owners, width), 1) + base) // cap == iota((owners, width), 0)).astype(F32).astype(BF16)


LANES = 128


def make_requests(owners, cap):
    def kernel(parent_ref, place_ref, tally_ref, table, rank_ref, rank_t_ref, ask_ref, table_low_ref, row_ref):
        slots, pairs = parent_ref.shape
        line = iota((LANES, pairs), 0)
        tally = tally_ref[...]
        named = jnp.zeros((LANES, pairs), F32)
        where = jnp.zeros((LANES, pairs), F32)
        for c in range(slots):
            hit = jnp.logical_and(parent_ref[c : c + 1, :] == line, tally > c)
            named = jnp.where(hit, 1.0, named)
            where = jnp.where(hit, place_ref[c : c + 1, :].astype(F32), where)
        before = (iota((pairs, pairs), 0) < iota((pairs, pairs), 1)).astype(F32).astype(BF16)
        rank_t = jnp.where(named > 0, mm(named.astype(BF16), before), -1.0)
        rank = rank_t.T
        rank_t_ref[...] = rank_t.astype(BF16)
        rank_ref[...] = rank.astype(BF16)
        where = where.T.astype(jnp.int32)
        high = (where // 64).astype(F32).astype(BF16)
        low = (where % 64).astype(F32).astype(BF16)
        rank = rank.astype(BF16)
        total = owners * cap
        width = 512
        for base in range(0, total, width):
            spread = expander(LANES, cap, base, width)
            want = (iota((pairs, width), 1) % cap).astype(F32)
            place = mm(high, spread) * 64.0 + mm(low, spread)
            row_ref[:, base : base + width] = jnp.sum(
                jnp.where(mm(rank, spread) == want, place, 0.0), axis=0, keepdims=True
            )
        for o in range(owners):
            ask = row_ref[:, o * cap : (o + 1) * cap].astype(jnp.int32)
            ask_ref[o, :, 0:cap] = jnp.broadcast_to(ask, (ask_ref.shape[1], cap))
        table_low_ref[...] = table.get()[...].astype(BF16)

    return kernel


def normalize(rows):
    radius = jnp.sqrt(jnp.sum(rows * rows, axis=1, keepdims=True) + epsilon)
    return rows / radius, radius


def unit_queries(query_ref, lines_ref, send_ref):
    pairs = query_ref.shape[0]
    slots = lines_ref.shape[0]
    unit, _ = normalize(query_ref[...].astype(F32))
    send_ref[0:pairs, :] = unit.astype(BF16)
    tail = send_ref.shape[0] - pairs
    line = iota((tail, pairs), 0)
    extra = jnp.zeros((tail, pairs), F32)
    for h in range(slots):
        row = lines_ref[h : h + 1, :]
        extra = jnp.where(line == h, (row // 64).astype(F32), extra)
        extra = jnp.where(line == h + slots, (row % 64).astype(F32), extra)
    send_ref[pairs:, :] = extra.astype(BF16)


def prepare(cap):
    def kernel(rank_ref, rank_t_ref, lines_ref, hot_ref, pick_ref, place_ref, hot_sum_ref, lines_t_ref):
        pairs = rank_ref.shape[0]
        slots = lines_ref.shape[0]
        width = pick_ref.shape[1]
        base = pl.program_id(0) * width

        @pl.when(pl.program_id(0) == 0)
        def _():
            hot_sum_ref[...] = jnp.zeros_like(hot_sum_ref)
            line = iota((LANES, pairs), 0)
            lines = jnp.zeros((LANES, pairs), F32)
            for h in range(slots):
                lines = jnp.where(line == h, lines_ref[h : h + 1, :].astype(F32), lines)
            lines_t_ref[...] = lines.T.astype(jnp.int32)

        spread = expander(LANES, cap, base, width)
        want = (iota((pairs, width), 1) % cap).astype(F32)
        pick_ref[...] = (mm(rank_ref[...], spread) == want).astype(F32).astype(BF16)
        spread_t = ((iota((width, LANES), 0) + base) // cap == iota((width, LANES), 1))
        want_t = (iota((width, pairs), 0) % cap).astype(F32)
        hit = mm(spread_t.astype(F32).astype(BF16), rank_t_ref[...]) == want_t
        place_ref[...] = hit.astype(F32).astype(BF16)
        column = iota((pairs, width), 1) + base
        counts = jnp.zeros((pairs, width), F32)
        for h in range(slots):
            counts += (lines_t_ref[:, h : h + 1] == column).astype(F32)
        hot_sum_ref[...] += mm(counts.astype(BF16), hot_ref[...])

    return kernel


def fetch(ask_ref, table_ref, out_ref):
    rows = table_ref.shape[0]
    group, cap = out_ref.shape[0], out_ref.shape[1]
    diagonal = iota((cap, cap), 0) == iota((cap, cap), 1)
    columns = []
    for g in range(group):
        ask = ask_ref[pl.program_id(0) * group + g, 0:1, 0:cap]
        columns.append(jnp.sum(jnp.where(diagonal, ask, 0).astype(F32), axis=1, keepdims=True))
    column = jnp.concatenate(columns, axis=0).astype(jnp.int32)
    hit = (column == iota((group * cap, rows), 1)).astype(F32).astype(BF16)
    out_ref[...] = mm(hit, table_ref[...]).astype(BF16).reshape(out_ref.shape)


def loss_side(own_low, others, total_ref, sharpness, additive):
    rows = own_low.shape[0]
    for i, late in enumerate(others):
        other = late.get()[...]
        grad = jax.nn.sigmoid(sharpness * mm(own_low, other, NT) + additive)
        if i == 0:
            grad = grad - (iota((rows, rows), 0) == iota((rows, rows), 1)).astype(F32)
            total_ref[...] = mm(grad.astype(BF16), other)
        else:
            total_ref[...] += mm(grad.astype(BF16), other)
    return sharpness * total_ref[...]


def project(unit, radius, direction):
    inner = jnp.sum(unit * direction, axis=1, keepdims=True)
    return (direction - unit * inner) / radius


def item_side(blocks):
    def kernel(sharp_ref, add_ref, fetched_ref, pick_ref, place, hot_sum, *refs):
        queries, (sides_ref, out_ref, total_ref, stage_ref, sem) = refs[:blocks], refs[blocks:]
        pairs = total_ref.shape[0]
        unit, radius = normalize(mm(pick_ref[...], fetched_ref[...]) + hot_sum.get()[...])
        low = unit.astype(BF16)
        sides_ref[0:pairs, :] = low
        direction = loss_side(low, queries, total_ref, sharp_ref[0], add_ref[0])
        grad = project(unit, radius, direction).astype(BF16)
        sides_ref[pairs:, :] = grad
        place_ref = place.get()
        steps = sem.shape[0]
        width = place_ref.shape[0] // steps

        def leave(i):
            part = pl.ds(pl.multiple_of(i * width, width), width)
            return pltpu.make_async_copy(stage_ref.at[part], out_ref.at[part], sem.at[i])

        def step(i, _):
            part = pl.ds(pl.multiple_of(i * width, width), width)
            stage_ref[part, :] = mm(place_ref[part, :], grad).astype(BF16)
            leave(i).start()
            return 0

        def finish(i, _):
            leave(i).wait()
            return 0

        lax.fori_loop(0, steps, step, 0)
        lax.fori_loop(0, steps, finish, 0)

    return kernel


def query_side(sharp_ref, add_ref, query_ref, *refs):
    items, (out_ref, total_ref) = refs[:-2], refs[-2:]
    unit, radius = normalize(query_ref[...].astype(F32))
    direction = loss_side(unit.astype(BF16), items, total_ref, sharp_ref[0], add_ref[0])
    out_ref[...] = project(unit, radius, direction)


def hot_terms(blocks, slots):
    def kernel(block_ref, *refs):
        grads, lines, (out_ref, total_ref) = refs[:blocks], refs[blocks : 2 * blocks], refs[2 * blocks :]
        width, pairs = out_ref.shape
        row = (iota((width, pairs), 0) + block_ref[0] * width).astype(F32)
        for i, (grad, line) in enumerate(zip(grads, lines)):
            line = line.get()[...].astype(F32)
            counts = jnp.zeros((width, pairs), F32)
            for h in range(slots):
                counts += (line[h : h + 1, :] * 64.0 + line[h + slots : h + slots + 1, :] == row).astype(F32)
            term = mm(counts.astype(BF16), grad.get()[...])
            total_ref[...] = term if i == 0 else total_ref[...] + term
        out_ref[...] = total_ref[...].astype(BF16)

    return kernel


def hot_sum_spread(parts_ref, out_ref):
    piece = jnp.sum(parts_ref[...].astype(F32), axis=0, keepdims=True)
    out_ref[...] = jnp.broadcast_to(piece, out_ref.shape).astype(BF16)


def widen(blocks):
    def kernel(block_ref, *refs):
        part_refs, out_ref = refs[:blocks], refs[blocks]
        chips = blocks // 2
        width = part_refs[0].shape[0]
        mine, core = block_ref[0] // 2, block_ref[0] % 2
        for i, ref in enumerate(part_refs):
            chip = (mine + chips - i % chips) % chips
            index = chip * 2 + (core if i < chips else 1 - core)
            out_ref[pl.ds(pl.multiple_of(index * width, width), width), :] = ref[...].astype(F32)

    return kernel


def cold_terms(same_core):
    def kernel(block_ref, ask_ref, grad_ref, out_ref, row_ref):
        width, total = out_ref.shape[1], grad_ref.shape[0]
        owners, chips = ask_ref.shape[0], pl.num_programs(0)
        cap = total // owners

        @pl.when(pl.program_id(0) == 0)
        def _():
            for o in range(owners):
                row_ref[:, o * cap : (o + 1) * cap] = ask_ref[o, 0:1, 0:cap]

        core = block_ref[0] % 2
        core = core if same_core else 1 - core
        chip = (block_ref[0] // 2 + pl.program_id(0)) % chips
        row = iota((width, total), 0) + (chip * 2 + core) * width
        hit = (row_ref[...] == row).astype(F32).astype(BF16)
        out_ref[0] = mm(hit, grad_ref[...]).astype(out_ref.dtype)

    return kernel


def cold_join(mine_ref, theirs_ref, keep_ref, *send_refs):
    keep_ref[...] = mine_ref[0] + theirs_ref[0].astype(F32)
    for d, ref in enumerate(send_refs):
        ref[...] = (mine_ref[d + 1] + theirs_ref[d + 1].astype(F32)).astype(BF16)


def add_parts(keep_ref, *refs):
    part_refs, out_ref = refs[:-1], refs[-1]
    total = keep_ref[...]
    for ref in part_refs:
        total += ref[...].astype(F32)
    out_ref[...] = total


def whole(array):
    rank = len(array.shape)
    return pl.BlockSpec(array.shape, lambda i: (0,) * rank)


def swap(array, axis):
    return lax.all_to_all(array, axis, split_axis=0, concat_axis=0, tiled=True)


def cross(array, blocks):
    return lax.ppermute(array, "blk", [(i, i ^ 1) for i in range(blocks)])


def shift(array, blocks, d):
    return lax.ppermute(array, "blk", [(i, (i + 2 * d) % blocks) for i in range(blocks)])


def gather_blocks(array, blocks):
    first = cross(array, blocks)
    mine = [shift(array, blocks, d) for d in range(1, blocks // 2)]
    return [array] + mine + [first] + [cross(m, blocks) for m in mine]


def step_of(queries, hot_table, cold_table, lines, parent, place, tally, sharpness, additive):
    pairs, width = queries.shape
    owners, blocks = lax.axis_size("shard"), lax.axis_size("blk")
    chips = blocks // 2
    slots = parent.shape[1]
    cap = 2 * pairs * slots // owners
    total = owners * cap
    rows = cold_table.shape[0]
    hot_rows = hot_table.shape[0]
    block = lax.axis_index("blk").astype(jnp.int32).reshape(1)

    rank, rank_t, ask, table_low = call(
        make_requests(owners, cap),
        [shape((pairs, LANES), BF16), shape((LANES, pairs), BF16), HBM((owners, 8, LANES), jnp.int32), shape((rows, width), BF16)],
        parent.T, place.T, tally.reshape(1, pairs), cold_table,
        kinds=["h", "h", "h", slice(0, rows)],
        scratch=[pltpu.VMEM((1, total), F32)],
        flops=2 * pairs * total * LANES * 3,
    )
    asked = swap(ask, "shard")

    group = 4
    (looked,) = call(
        fetch,
        [HBM((owners, cap, width), BF16)],
        asked, table_low,
        grid=(owners // group,),
        out_specs=[pl.BlockSpec((group, cap, width), lambda i: (i, 0, 0))],
        flops=2 * total * rows * width,
    )
    looked, queries, rank, rank_t = lax.optimization_barrier((looked, queries, rank, rank_t))
    fetched = swap(looked, "shard").reshape(total, width)

    lines_t = lines.T
    (query_block,) = call(unit_queries, [HBM((pairs + 16, width), BF16)], queries, lines_t, kinds=["h", "h"])
    query_blocks = gather_blocks(query_block, blocks)

    step = 256
    pick, placed, hot_sum = call(
        prepare(cap),
        [shape((pairs, total), BF16), HBM((total, pairs), BF16), HBM((pairs, width), F32)],
        rank, rank_t, lines_t, hot_table,
        kinds=["v", "v", "h", "h"],
        grid=(total // step,),
        in_specs=[whole(rank), whole(rank_t), whole(lines_t), pl.BlockSpec((hot_rows * step // total, width), lambda i: (i, 0))],
        out_specs=[
            pl.BlockSpec((pairs, step), lambda i: (0, i)),
            pl.BlockSpec((step, pairs), lambda i: (i, 0)),
            pl.BlockSpec((pairs, width), lambda i: (0, 0)),
        ],
        scratch=[pltpu.VMEM((pairs, LANES), jnp.int32)],
        flops=2 * pairs * total * (width + 2 * LANES),
    )

    mine, after, tail = slice(0, pairs), slice(pairs, 2 * pairs), slice(pairs, pairs + 16)
    steps = 8
    sides, outgoing = call(
        item_side(blocks),
        [HBM((2 * pairs, width), BF16), HBM((total, width), BF16)],
        sharpness, additive, fetched, pick, placed, hot_sum, *query_blocks,
        kinds=["s", "s", "v", "v", slice(0, total), mine] + [mine] * blocks,
        out_specs=[pl.BlockSpec((2 * pairs, width), lambda i: (0, 0)), pl.BlockSpec(memory_space=HBM)],
        scratch=[
            pltpu.VMEM((pairs, width), F32),
            pltpu.VMEM((total, width), BF16),
            pltpu.SemaphoreType.DMA((steps,)),
        ],
        flops=2 * pairs * width * (2 * total + 2 * blocks * pairs),
    )
    incoming = swap(outgoing.reshape(owners, cap, width), "shard").reshape(total, width)

    side_blocks = gather_blocks(sides, blocks)
    (hot_block,) = call(
        hot_terms(blocks, slots),
        [HBM((hot_rows // blocks, width), BF16)],
        block, *side_blocks, *query_blocks,
        kinds=["s"] + [after] * blocks + [tail] * blocks,
        scratch=[pltpu.VMEM((hot_rows // blocks, width), F32)],
        flops=2 * blocks * pairs * width * hot_rows // blocks,
    )
    (query_grad,) = call(
        query_side,
        [HBM((pairs, width), F32)],
        sharpness, additive, queries, *side_blocks,
        kinds=["s", "s", "h"] + [mine] * blocks,
        scratch=[pltpu.VMEM((pairs, width), F32)],
        flops=4 * pairs * width * blocks * pairs,
    )
    hot_parts = swap(hot_block.reshape(owners, hot_rows // blocks // owners, width), "shard")
    (hot_piece,) = call(hot_sum_spread, [HBM(hot_parts.shape, BF16)], hot_parts)

    def cold_half(same_core, dtype, incoming):
        return call(
            cold_terms(same_core),
            [shape((chips, rows // blocks, width), dtype)],
            block, asked, incoming,
            kinds=["s", "v", "v"],
            grid=(chips,),
            out_specs=[pl.BlockSpec((1, rows // blocks, width), lambda i: (i, 0, 0))],
            scratch=[pltpu.VMEM((1, total), jnp.int32)],
            flops=total * rows * width,
        )[0]

    theirs = cold_half(False, BF16, incoming)
    theirs = cross(theirs, blocks)
    mine = cold_half(True, F32, incoming)
    keep, *sends = call(
        cold_join,
        [shape((rows // blocks, width), F32)] + [shape((rows // blocks, width), BF16)] * (chips - 1),
        mine, theirs,
    )
    hot_block = swap(hot_piece, "shard").reshape(hot_rows // blocks, width)
    parts = [shift(part, blocks, d + 1) for d, part in enumerate(sends)]
    (cold_grad,) = call(add_parts, [HBM((rows // blocks, width), F32)], keep, *parts)
    hot_blocks = gather_blocks(hot_block, blocks)
    (hot_grad,) = call(widen(blocks), [HBM((hot_rows, width), F32)], block, *hot_blocks, kinds=["s"] + ["v"] * blocks)
    return (query_grad, hot_grad, cold_grad)


def solution(mesh):
    pair = P(("shard", "blk"), None)
    in_specs = (pair, P(), P("shard", None), pair, pair, pair, P(("shard", "blk")), P(), P())
    return jax.shard_map(step_of, mesh=mesh, in_specs=in_specs, out_specs=(pair, P(), pair), check_vma=False)
```

```python
import jax
import jax.numpy as jnp
from jax import lax
from jax.experimental import pallas as pl
from jax.experimental.pallas import tpu as pltpu
from jax.sharding import PartitionSpec as P


epsilon = 1e-06
F32 = jnp.float32
BF16 = jnp.bfloat16
NN = (((1,), (0,)), ((), ()))
NT = (((1,), (1,)), ((), ()))


def mm(a, b, dims=NN):
    return lax.dot_general(a, b, dims, preferred_element_type=F32)


def iota(shape, dim):
    return lax.broadcasted_iota(jnp.int32, shape, dim)


HBM = pltpu.HBM


class Late:
    def __init__(self, source, buffer, sem):
        self.copy = pltpu.make_async_copy(source, buffer, sem)
        self.buffer = buffer
        self.copy.start()
        self.waits = True

    def get(self):
        if self.waits:
            self.copy.wait()
            self.waits = False
        return self.buffer


class Leave:
    def __init__(self, out_ref, stage_ref, sem):
        self.out, self.stage, self.sem = out_ref, stage_ref, sem
        self.steps = sem.shape[0]
        self.width = stage_ref.shape[0] // self.steps

    def copy(self, i):
        part = pl.ds(i * self.width, self.width)
        return pltpu.make_async_copy(self.stage.at[part], self.out.at[part], self.sem.at[i])

    def run(self, compute):
        def step(i, _):
            self.stage[pl.ds(i * self.width, self.width)] = compute(i)
            self.copy(i).start()
            return 0

        def finish(i, _):
            self.copy(i).wait()
            return 0

        lax.fori_loop(0, self.steps, step, 0)
        lax.fori_loop(0, self.steps, finish, 0)


def call(kernel, outs, *args, kinds=None, scratch=(), flops=0, grid=(1,), in_specs=None, out_specs=None):
    kinds = kinds or ["v"] * len(args)
    near = [isinstance(kind, tuple) for kind in kinds]
    kinds = [kind[0] if isinstance(kind, tuple) else kind for kind in kinds]
    late = [k for k, kind in enumerate(kinds) if isinstance(kind, slice)]
    specs, operands = [], []
    for k, (kind, arg) in enumerate(zip(kinds, args)):
        if kind == "s":
            specs.append(pl.BlockSpec(memory_space=pltpu.SMEM))
        elif k in late:
            specs.append(pl.BlockSpec(memory_space=pl.ANY if near[k] else HBM))
            if not near[k]:
                arg = pltpu.with_memory_space_constraint(arg, HBM)
        else:
            specs.append(in_specs[k] if in_specs else whole(arg))
            if kind == "h":
                arg = pltpu.with_memory_space_constraint(arg, HBM)
        operands.append(arg)
    buffers = []
    for k in late:
        rows = kinds[k].stop - kinds[k].start
        buffers.append(pltpu.VMEM((rows,) + args[k].shape[1:], args[k].dtype))

    def run(*refs):
        refs, extra = list(refs[: len(refs) - len(late) - 1]), refs[len(refs) - len(late) - 1 :]
        for n, k in enumerate(late):
            refs[k] = Late(refs[k].at[kinds[k]], extra[n], extra[-1].at[n])
        kernel(*refs)

    moved = sum(a.size * a.dtype.itemsize for a in args)
    return pl.pallas_call(
        run if late else kernel,
        out_shape=list(outs),
        grid=grid,
        in_specs=specs,
        out_specs=out_specs or [whole(o) for o in outs],
        scratch_shapes=list(scratch) + (buffers + [pltpu.SemaphoreType.DMA((len(late),))] if late else []),
        compiler_params=pltpu.CompilerParams(vmem_limit_bytes=24 << 20),
        cost_estimate=pl.CostEstimate(flops=flops, bytes_accessed=moved, transcendentals=0),
    )(*operands)


def shape(dims, dtype):
    return jax.ShapeDtypeStruct(dims, dtype)


def expander(owners, cap, base, width):
    return ((iota((owners, width), 1) + base) // cap == iota((owners, width), 0)).astype(F32).astype(BF16)


LANES = 128


def make_requests(owners, cap):
    def kernel(parent_ref, place_ref, tally_ref, table, rank_ref, rank_t_ref, ask_ref, table_low_ref, row_ref):
        slots, pairs = parent_ref.shape
        line = iota((LANES, pairs), 0)
        tally = tally_ref[...]
        named = jnp.zeros((LANES, pairs), F32)
        where = jnp.zeros((LANES, pairs), F32)
        for c in range(slots):
            hit = jnp.logical_and(parent_ref[c : c + 1, :] == line, tally > c)
            named = jnp.where(hit, 1.0, named)
            where = jnp.where(hit, place_ref[c : c + 1, :].astype(F32), where)
        before = (iota((pairs, pairs), 0) < iota((pairs, pairs), 1)).astype(F32).astype(BF16)
        rank_t = jnp.where(named > 0, mm(named.astype(BF16), before), -1.0)
        rank = rank_t.T
        rank_t_ref[...] = rank_t.astype(BF16)
        rank_ref[...] = rank.astype(BF16)
        where = where.T.astype(jnp.int32)
        high = (where // 64).astype(F32).astype(BF16)
        low = (where % 64).astype(F32).astype(BF16)
        rank = rank.astype(BF16)
        total = owners * cap
        width = 512
        for base in range(0, total, width):
            spread = expander(LANES, cap, base, width)
            want = (iota((pairs, width), 1) % cap).astype(F32)
            place = mm(high, spread) * 64.0 + mm(low, spread)
            row_ref[:, base : base + width] = jnp.sum(
                jnp.where(mm(rank, spread) == want, place, 0.0), axis=0, keepdims=True
            )
        for o in range(owners):
            ask = row_ref[:, o * cap : (o + 1) * cap].astype(jnp.int32)
            ask_ref[o, :, 0:cap] = jnp.broadcast_to(ask, (ask_ref.shape[1], cap))
        table_low_ref[...] = table.get()[...].astype(BF16)

    return kernel


def normalize(rows):
    radius = jnp.sqrt(jnp.sum(rows * rows, axis=1, keepdims=True) + epsilon)
    return rows / radius, radius


def unit_queries(query_ref, lines_ref, send_ref):
    pairs = query_ref.shape[0]
    slots = lines_ref.shape[0]
    unit, _ = normalize(query_ref[...].astype(F32))
    send_ref[0:pairs, :] = unit.astype(BF16)
    tail = send_ref.shape[0] - pairs
    line = iota((tail, pairs), 0)
    extra = jnp.zeros((tail, pairs), F32)
    for h in range(slots):
        row = lines_ref[h : h + 1, :]
        extra = jnp.where(line == h, (row // 64).astype(F32), extra)
        extra = jnp.where(line == h + slots, (row % 64).astype(F32), extra)
    send_ref[pairs:, :] = extra.astype(BF16)


def prepare(cap):
    def kernel(rank_ref, rank_t_ref, lines_ref, hot, pick_ref, out_ref, hot_sum_ref, stage_ref, sem):
        pairs = rank_ref.shape[0]
        slots = lines_ref.shape[0]
        rank, rank_t = rank_ref[...], rank_t_ref[...]
        line = iota((LANES, pairs), 0)
        lines = jnp.zeros((LANES, pairs), F32)
        for h in range(slots):
            lines = jnp.where(line == h, lines_ref[h : h + 1, :].astype(F32), lines)
        lines = lines.T.astype(jnp.int32)
        leave = Leave(out_ref, stage_ref, sem)
        width = leave.width
        want = (iota((pairs, width), 1) % cap).astype(F32)
        want_t = (iota((width, pairs), 0) % cap).astype(F32)
        hot_ref = hot.get()
        hot_sum_ref[...] = jnp.zeros_like(hot_sum_ref)

        def compute(i):
            base = pl.multiple_of(i * width, width)
            spread = expander(LANES, cap, base, width)
            pick_ref[:, pl.ds(base, width)] = (mm(rank, spread) == want).astype(F32).astype(BF16)
            column = iota((pairs, width), 1) + base
            counts = jnp.zeros((pairs, width), F32)
            for h in range(slots):
                counts += (lines[:, h : h + 1] == column).astype(F32)
            hot_sum_ref[...] += mm(counts.astype(BF16), hot_ref[pl.ds(base, width), :])
            spread_t = ((iota((width, LANES), 0) + base) // cap == iota((width, LANES), 1))
            hit = mm(spread_t.astype(F32).astype(BF16), rank_t) == want_t
            return hit.astype(F32).astype(BF16)

        leave.run(compute)

    return kernel


def fetch(ask_ref, table_ref, out_ref, stage_ref, sem):
    rows = table_ref.shape[0]
    cap = stage_ref.shape[1]
    leave = Leave(out_ref, stage_ref, sem)
    group = leave.width
    diagonal = iota((cap, cap), 0) == iota((cap, cap), 1)
    lane = iota((group * cap, rows), 1)

    def compute(i):
        columns = []
        for g in range(group):
            ask = ask_ref[i * group + g, 0:1, 0:cap]
            columns.append(jnp.sum(jnp.where(diagonal, ask, 0).astype(F32), axis=1, keepdims=True))
        column = jnp.concatenate(columns, axis=0).astype(jnp.int32)
        hit = (column == lane).astype(F32).astype(BF16)
        return mm(hit, table_ref[...]).astype(BF16).reshape(group, cap, table_ref.shape[1])

    leave.run(compute)


def loss_side(own_low, others, total_ref, sharpness, additive):
    rows = own_low.shape[0]
    for i, late in enumerate(others):
        other = late.get()[0:rows, :]
        grad = jax.nn.sigmoid(sharpness * mm(own_low, other, NT) + additive)
        if i == 0:
            grad = grad - (iota((rows, rows), 0) == iota((rows, rows), 1)).astype(F32)
            total_ref[...] = mm(grad.astype(BF16), other)
        else:
            total_ref[...] += mm(grad.astype(BF16), other)
    return sharpness * total_ref[...]


def project(unit, radius, direction):
    inner = jnp.sum(unit * direction, axis=1, keepdims=True)
    return (direction - unit * inner) / radius


def item_side(blocks):
    def kernel(sharp_ref, add_ref, fetched_ref, pick_ref, hot_sum, *refs):
        queries, place = refs[:blocks], refs[blocks]
        sides_ref, tails_ref, out_ref, total_ref, stage_ref, sem = refs[blocks + 1 :]
        pairs = total_ref.shape[0]
        unit, radius = normalize(mm(pick_ref[...], fetched_ref[...]) + hot_sum.get()[...])
        low = unit.astype(BF16)
        sides_ref[0:pairs, :] = low
        direction = loss_side(low, queries, total_ref, sharp_ref[0], add_ref[0])
        for i, query in enumerate(queries):
            tails_ref[i] = query.get()[pairs:, :]
        grad = project(unit, radius, direction).astype(BF16)
        sides_ref[pairs:, :] = grad
        place_ref = place.get()
        leave = Leave(out_ref, stage_ref, sem)
        leave.run(lambda i: mm(place_ref[pl.ds(i * leave.width, leave.width), :], grad).astype(BF16))

    return kernel


def query_side(sharp_ref, add_ref, query_ref, *refs):
    items, (out_ref, total_ref) = refs[:-2], refs[-2:]
    unit, radius = normalize(query_ref[...].astype(F32))
    direction = loss_side(unit.astype(BF16), items, total_ref, sharp_ref[0], add_ref[0])
    out_ref[...] = project(unit, radius, direction)


def hot_terms(blocks, slots):
    def kernel(block_ref, lines_ref, *refs):
        grads, (out_ref, total_ref) = refs[:blocks], refs[blocks:]
        width, pairs = out_ref.shape
        row = (iota((width, pairs), 0) + block_ref[0] * width).astype(F32)
        for i, grad in enumerate(grads):
            line = lines_ref[i].astype(F32)
            counts = jnp.zeros((width, pairs), F32)
            for h in range(slots):
                counts += (line[h : h + 1, :] * 64.0 + line[h + slots : h + slots + 1, :] == row).astype(F32)
            term = mm(counts.astype(BF16), grad.get()[...])
            total_ref[...] = term if i == 0 else total_ref[...] + term
        out_ref[...] = total_ref[...].astype(BF16)

    return kernel


def hot_sum_spread(parts_ref, out_ref):
    piece = jnp.sum(parts_ref[...].astype(F32), axis=0, keepdims=True)
    out_ref[...] = jnp.broadcast_to(piece, out_ref.shape).astype(BF16)


def widen(blocks):
    def kernel(block_ref, *refs):
        part_refs, out_ref = refs[:blocks], refs[blocks]
        chips = blocks // 2
        width = part_refs[0].shape[0]
        mine, core = block_ref[0] // 2, block_ref[0] % 2
        for i, ref in enumerate(part_refs):
            chip = (mine + chips - i % chips) % chips
            index = chip * 2 + (core if i < chips else 1 - core)
            out_ref[pl.ds(pl.multiple_of(index * width, width), width), :] = ref[...].astype(F32)

    return kernel


def cold_terms(same_core):
    def kernel(block_ref, ask_ref, grad_ref, out_ref, row_ref):
        width, total = out_ref.shape[1], grad_ref.shape[0]
        owners, chips = ask_ref.shape[0], pl.num_programs(0)
        cap = total // owners

        @pl.when(pl.program_id(0) == 0)
        def _():
            for o in range(owners):
                row_ref[:, o * cap : (o + 1) * cap] = ask_ref[o, 0:1, 0:cap]

        core = block_ref[0] % 2
        core = core if same_core else 1 - core
        chip = (block_ref[0] // 2 + pl.program_id(0)) % chips
        row = iota((width, total), 0) + (chip * 2 + core) * width
        hit = (row_ref[...] == row).astype(F32).astype(BF16)
        out_ref[0] = mm(hit, grad_ref[...]).astype(out_ref.dtype)

    return kernel


def cold_join(mine_ref, theirs_ref, keep_ref, *send_refs):
    keep_ref[...] = mine_ref[0] + theirs_ref[0].astype(F32)
    for d, ref in enumerate(send_refs):
        ref[...] = (mine_ref[d + 1] + theirs_ref[d + 1].astype(F32)).astype(BF16)


def add_parts(keep_ref, *refs):
    part_refs, out_ref = refs[:-1], refs[-1]
    total = keep_ref[...]
    for ref in part_refs:
        total += ref[...].astype(F32)
    out_ref[...] = total


def whole(array):
    rank = len(array.shape)
    return pl.BlockSpec(array.shape, lambda i: (0,) * rank)


def swap(array, axis):
    return lax.all_to_all(array, axis, split_axis=0, concat_axis=0, tiled=True)


def cross(array, blocks):
    return lax.ppermute(array, "blk", [(i, i ^ 1) for i in range(blocks)])


def shift(array, blocks, d):
    return lax.ppermute(array, "blk", [(i, (i + 2 * d) % blocks) for i in range(blocks)])


def gather_blocks(array, blocks):
    first = cross(array, blocks)
    mine = [shift(array, blocks, d) for d in range(1, blocks // 2)]
    return [array] + mine + [first] + [cross(m, blocks) for m in mine]


def step_of(queries, hot_table, cold_table, lines, parent, place, tally, sharpness, additive):
    pairs, width = queries.shape
    owners, blocks = lax.axis_size("shard"), lax.axis_size("blk")
    chips = blocks // 2
    slots = parent.shape[1]
    cap = 2 * pairs * slots // owners
    total = owners * cap
    rows = cold_table.shape[0]
    hot_rows = hot_table.shape[0]
    block = lax.axis_index("blk").astype(jnp.int32).reshape(1)

    rank, rank_t, ask, table_low = call(
        make_requests(owners, cap),
        [shape((pairs, LANES), BF16), shape((LANES, pairs), BF16), HBM((owners, 8, LANES), jnp.int32), shape((rows, width), BF16)],
        parent.T, place.T, tally.reshape(1, pairs), cold_table,
        kinds=["h", "h", "h", slice(0, rows)],
        scratch=[pltpu.VMEM((1, total), F32)],
        flops=2 * pairs * total * LANES * 3,
    )
    asked = swap(ask, "shard")

    steps = 8
    (looked,) = call(
        fetch,
        [HBM((owners, cap, width), BF16)],
        asked, table_low,
        out_specs=[pl.BlockSpec(memory_space=HBM)],
        scratch=[pltpu.VMEM((owners, cap, width), BF16), pltpu.SemaphoreType.DMA((steps,))],
        flops=2 * total * rows * width,
    )
    looked, queries, rank, rank_t = lax.optimization_barrier((looked, queries, rank, rank_t))
    fetched = swap(looked, "shard").reshape(total, width)

    lines_t = lines.T
    (query_block,) = call(unit_queries, [HBM((pairs + 16, width), BF16)], queries, lines_t, kinds=["h", "h"])
    query_blocks = gather_blocks(query_block, blocks)

    pick, placed, hot_sum = call(
        prepare(cap),
        [shape((pairs, total), BF16), HBM((total, pairs), BF16), HBM((pairs, width), F32)],
        rank, rank_t, lines_t, hot_table,
        kinds=["v", "v", "h", slice(0, hot_rows)],
        out_specs=[
            pl.BlockSpec((pairs, total), lambda i: (0, 0)),
            pl.BlockSpec(memory_space=HBM),
            pl.BlockSpec((pairs, width), lambda i: (0, 0)),
        ],
        scratch=[pltpu.VMEM((total, pairs), BF16), pltpu.SemaphoreType.DMA((steps,))],
        flops=2 * pairs * total * (width + 2 * LANES),
    )

    mine, after, block_rows = slice(0, pairs), slice(pairs, 2 * pairs), slice(0, pairs + 16)
    sides, tails, outgoing = call(
        item_side(blocks),
        [HBM((2 * pairs, width), BF16), shape((blocks, 16, width), BF16), HBM((total, width), BF16)],
        sharpness, additive, fetched, pick, hot_sum, *query_blocks, placed,
        kinds=["s", "s", "v", "v", mine, block_rows] + [(block_rows,)] * (blocks - 1) + [slice(0, total)],
        out_specs=[
            pl.BlockSpec((2 * pairs, width), lambda i: (0, 0)),
            pl.BlockSpec((blocks, 16, width), lambda i: (0, 0, 0)),
            pl.BlockSpec(memory_space=HBM),
        ],
        scratch=[
            pltpu.VMEM((pairs, width), F32),
            pltpu.VMEM((total, width), BF16),
            pltpu.SemaphoreType.DMA((steps,)),
        ],
        flops=2 * pairs * width * (2 * total + 2 * blocks * pairs),
    )
    incoming = swap(outgoing.reshape(owners, cap, width), "shard").reshape(total, width)

    side_blocks = gather_blocks(sides, blocks)
    (hot_block,) = call(
        hot_terms(blocks, slots),
        [HBM((hot_rows // blocks, width), BF16)],
        block, tails, *side_blocks,
        kinds=["s", "v", after] + [(after,)] * (blocks - 1),
        scratch=[pltpu.VMEM((hot_rows // blocks, width), F32)],
        flops=2 * blocks * pairs * width * hot_rows // blocks,
    )
    (query_grad,) = call(
        query_side,
        [HBM((pairs, width), F32)],
        sharpness, additive, queries, *side_blocks,
        kinds=["s", "s", "h", mine] + [(mine,)] * (blocks - 1),
        scratch=[pltpu.VMEM((pairs, width), F32)],
        flops=4 * pairs * width * blocks * pairs,
    )
    hot_parts = swap(hot_block.reshape(owners, hot_rows // blocks // owners, width), "shard")
    (hot_piece,) = call(hot_sum_spread, [HBM(hot_parts.shape, BF16)], hot_parts)

    def cold_half(same_core, dtype, incoming):
        return call(
            cold_terms(same_core),
            [shape((chips, rows // blocks, width), dtype)],
            block, asked, incoming,
            kinds=["s", "v", "v"],
            grid=(chips,),
            out_specs=[pl.BlockSpec((1, rows // blocks, width), lambda i: (i, 0, 0))],
            scratch=[pltpu.VMEM((1, total), jnp.int32)],
            flops=total * rows * width,
        )[0]

    theirs = cold_half(False, BF16, incoming)
    theirs = cross(theirs, blocks)
    mine = cold_half(True, F32, incoming)
    keep, *sends = call(
        cold_join,
        [shape((rows // blocks, width), F32)] + [shape((rows // blocks, width), BF16)] * (chips - 1),
        mine, theirs,
    )
    hot_block = swap(hot_piece, "shard").reshape(hot_rows // blocks, width)
    parts = [shift(part, blocks, d + 1) for d, part in enumerate(sends)]
    (cold_grad,) = call(add_parts, [HBM((rows // blocks, width), F32)], keep, *parts)
    hot_blocks = gather_blocks(hot_block, blocks)
    (hot_grad,) = call(widen(blocks), [HBM((hot_rows, width), F32)], block, *hot_blocks, kinds=["s"] + ["v"] * blocks)
    return (query_grad, hot_grad, cold_grad)


def solution(mesh):
    pair = P(("shard", "blk"), None)
    in_specs = (pair, P(), P("shard", None), pair, pair, pair, P(("shard", "blk")), P(), P())
    return jax.shard_map(step_of, mesh=mesh, in_specs=in_specs, out_specs=(pair, P(), pair), check_vma=False)
```

```python
import jax
import jax.numpy as jnp
from jax import lax
from jax.experimental import pallas as pl
from jax.experimental.pallas import tpu as pltpu
from jax.sharding import PartitionSpec as P


epsilon = 1e-06
F32 = jnp.float32
BF16 = jnp.bfloat16
NN = (((1,), (0,)), ((), ()))
NT = (((1,), (1,)), ((), ()))


def mm(a, b, dims=NN):
    return lax.dot_general(a, b, dims, preferred_element_type=F32)


def iota(shape, dim):
    return lax.broadcasted_iota(jnp.int32, shape, dim)


HBM = pltpu.HBM


class Late:
    def __init__(self, source, buffer, sem):
        self.copy = pltpu.make_async_copy(source, buffer, sem)
        self.buffer = buffer
        self.copy.start()
        self.waits = True

    def get(self):
        if self.waits:
            self.copy.wait()
            self.waits = False
        return self.buffer


class Leave:
    def __init__(self, out_ref, stage_ref, sem):
        self.out, self.stage, self.sem = out_ref, stage_ref, sem
        self.steps = sem.shape[0]
        self.width = stage_ref.shape[0] // self.steps

    def copy(self, i):
        part = pl.ds(i * self.width, self.width)
        return pltpu.make_async_copy(self.stage.at[part], self.out.at[part], self.sem.at[i])

    def write(self, value):
        self.stage[...] = value
        self.start()

    def start(self):
        for i in range(self.steps):
            self.copy(i).start()

    def finish(self):
        for i in range(self.steps):
            self.copy(i).wait()

    def run(self, compute):
        def step(i, _):
            self.stage[pl.ds(i * self.width, self.width)] = compute(i)
            self.copy(i).start()
            return 0

        def finish(i, _):
            self.copy(i).wait()
            return 0

        lax.fori_loop(0, self.steps, step, 0)
        lax.fori_loop(0, self.steps, finish, 0)


def call(kernel, outs, *args, kinds=None, scratch=(), flops=0, steps=1):
    kinds = kinds or ["v"] * len(args)
    late = [k for k, kind in enumerate(kinds) if kind == "h" or isinstance(kind, slice)]
    leaves = [k for k, out in enumerate(outs) if not isinstance(out, jax.ShapeDtypeStruct)]
    operands = [pltpu.with_memory_space_constraint(a, HBM) if k in late else a for k, a in enumerate(args)]
    spaces = [pltpu.SMEM if kind == "s" else HBM if k in late else pltpu.VMEM for k, kind in enumerate(kinds)]
    buffers = []
    for k in late:
        rows = args[k].shape[0] if kinds[k] == "h" else kinds[k].stop - kinds[k].start
        buffers += [pltpu.VMEM((rows,) + args[k].shape[1:], args[k].dtype), pltpu.SemaphoreType.DMA]
    for k in leaves:
        buffers += [pltpu.VMEM(outs[k].shape, outs[k].dtype), pltpu.SemaphoreType.DMA((steps,))]

    def run(*refs):
        refs, extra = list(refs[: len(refs) - len(buffers)]), list(refs[len(refs) - len(buffers) :])
        for k in late:
            source = refs[k] if kinds[k] == "h" else refs[k].at[kinds[k]]
            refs[k] = Late(source, extra.pop(0), extra.pop(0))
        for k in leaves:
            refs[len(args) + k] = Leave(refs[len(args) + k], extra.pop(0), extra.pop(0))
        kernel(*refs)

    moved = sum(a.size * a.dtype.itemsize for a in args)
    return pl.pallas_call(
        run,
        out_shape=list(outs),
        in_specs=[pl.BlockSpec(memory_space=space) for space in spaces],
        out_specs=[pl.BlockSpec(memory_space=HBM if k in leaves else pltpu.VMEM) for k in range(len(outs))],
        scratch_shapes=list(scratch) + buffers,
        compiler_params=pltpu.CompilerParams(vmem_limit_bytes=24 << 20),
        cost_estimate=pl.CostEstimate(flops=flops, bytes_accessed=moved, transcendentals=0),
    )(*operands)


def shape(dims, dtype):
    return jax.ShapeDtypeStruct(dims, dtype)


def expander(owners, cap, base, width):
    return ((iota((owners, width), 1) + base) // cap == iota((owners, width), 0)).astype(F32).astype(BF16)


LANES = 128


def make_requests(owners, cap):
    def kernel(parent, place, tally, table, rank_ref, rank_t_ref, ask, table_low_ref, row_ref):
        parent_ref, place_ref = parent.get(), place.get()
        slots, pairs = parent_ref.shape
        line = iota((LANES, pairs), 0)
        tally = tally.get()[...]
        named = jnp.zeros((LANES, pairs), F32)
        where = jnp.zeros((LANES, pairs), F32)
        for c in range(slots):
            hit = jnp.logical_and(parent_ref[c : c + 1, :] == line, tally > c)
            named = jnp.where(hit, 1.0, named)
            where = jnp.where(hit, place_ref[c : c + 1, :].astype(F32), where)
        before = (iota((pairs, pairs), 0) < iota((pairs, pairs), 1)).astype(F32).astype(BF16)
        rank_t = jnp.where(named > 0, mm(named.astype(BF16), before), -1.0)
        rank = rank_t.T
        rank_t_ref[...] = rank_t.astype(BF16)
        rank_ref[...] = rank.astype(BF16)
        where = where.T.astype(jnp.int32)
        high = (where // 64).astype(F32).astype(BF16)
        low = (where % 64).astype(F32).astype(BF16)
        rank = rank.astype(BF16)
        total = owners * cap
        width = 512
        for base in range(0, total, width):
            spread = expander(LANES, cap, base, width)
            want = (iota((pairs, width), 1) % cap).astype(F32)
            place = mm(high, spread) * 64.0 + mm(low, spread)
            row_ref[:, base : base + width] = jnp.sum(
                jnp.where(mm(rank, spread) == want, place, 0.0), axis=0, keepdims=True
            )
        for o in range(owners):
            row = row_ref[:, o * cap : (o + 1) * cap].astype(jnp.int32)
            ask.stage[o, :, 0:cap] = jnp.broadcast_to(row, (ask.stage.shape[1], cap))
        ask.start()
        table_low_ref[...] = table.get()[...].astype(BF16)
        ask.finish()

    return kernel


def normalize(rows):
    radius = jnp.sqrt(jnp.sum(rows * rows, axis=1, keepdims=True) + epsilon)
    return rows / radius, radius


def unit_queries(query, lines, send_ref):
    query_ref, lines_ref = query.get(), lines.get()
    pairs = query_ref.shape[0]
    slots = lines_ref.shape[0]
    unit, _ = normalize(query_ref[...].astype(F32))
    send_ref[0:pairs, :] = unit.astype(BF16)
    tail = send_ref.shape[0] - pairs
    line = iota((tail, pairs), 0)
    extra = jnp.zeros((tail, pairs), F32)
    for h in range(slots):
        row = lines_ref[h : h + 1, :]
        extra = jnp.where(line == h, (row // 64).astype(F32), extra)
        extra = jnp.where(line == h + slots, (row % 64).astype(F32), extra)
    send_ref[pairs:, :] = extra.astype(BF16)


def prepare(cap):
    def kernel(rank_ref, rank_t_ref, lines, hot, pick_ref, placed, hot_sum):
        lines_ref = lines.get()
        pairs = rank_ref.shape[0]
        slots = lines_ref.shape[0]
        rank, rank_t = rank_ref[...], rank_t_ref[...]
        line = iota((LANES, pairs), 0)
        lines = jnp.zeros((LANES, pairs), F32)
        for h in range(slots):
            lines = jnp.where(line == h, lines_ref[h : h + 1, :].astype(F32), lines)
        lines = lines.T.astype(jnp.int32)
        width = placed.width
        want = (iota((pairs, width), 1) % cap).astype(F32)
        want_t = (iota((width, pairs), 0) % cap).astype(F32)
        hot_ref = hot.get()
        hot_sum_ref = hot_sum.stage
        hot_sum_ref[...] = jnp.zeros_like(hot_sum_ref)

        def compute(i):
            base = pl.multiple_of(i * width, width)
            spread = expander(LANES, cap, base, width)
            pick_ref[:, pl.ds(base, width)] = (mm(rank, spread) == want).astype(F32).astype(BF16)
            column = iota((pairs, width), 1) + base
            counts = jnp.zeros((pairs, width), F32)
            for h in range(slots):
                counts += (lines[:, h : h + 1] == column).astype(F32)
            hot_sum_ref[...] += mm(counts.astype(BF16), hot_ref[pl.ds(base, width), :])
            spread_t = ((iota((width, LANES), 0) + base) // cap == iota((width, LANES), 1))
            hit = mm(spread_t.astype(F32).astype(BF16), rank_t) == want_t
            return hit.astype(F32).astype(BF16)

        placed.run(compute)
        hot_sum.start()
        hot_sum.finish()

    return kernel


def fetch(ask_ref, table_ref, out):
    rows = table_ref.shape[0]
    cap = out.stage.shape[1]
    group = out.width
    diagonal = iota((cap, cap), 0) == iota((cap, cap), 1)
    lane = iota((group * cap, rows), 1)

    def compute(i):
        columns = []
        for g in range(group):
            ask = ask_ref[i * group + g, 0:1, 0:cap]
            columns.append(jnp.sum(jnp.where(diagonal, ask, 0).astype(F32), axis=1, keepdims=True))
        column = jnp.concatenate(columns, axis=0).astype(jnp.int32)
        hit = (column == lane).astype(F32).astype(BF16)
        return mm(hit, table_ref[...]).astype(BF16).reshape(group, cap, table_ref.shape[1])

    out.run(compute)


def loss_side(own_low, other_refs, total_ref, sharpness, additive):
    rows = own_low.shape[0]
    for i, ref in enumerate(other_refs):
        other = ref[0:rows, :]
        grad = jax.nn.sigmoid(sharpness * mm(own_low, other, NT) + additive)
        if i == 0:
            grad = grad - (iota((rows, rows), 0) == iota((rows, rows), 1)).astype(F32)
            total_ref[...] = mm(grad.astype(BF16), other)
        else:
            total_ref[...] += mm(grad.astype(BF16), other)
    return sharpness * total_ref[...]


def project(unit, radius, direction):
    inner = jnp.sum(unit * direction, axis=1, keepdims=True)
    return (direction - unit * inner) / radius


def item_side(blocks):
    def kernel(sharp_ref, add_ref, fetched_ref, pick_ref, hot_sum, place, own, *refs):
        query_refs, refs = refs[: blocks - 1], refs[blocks - 1 :]
        (sides_ref, tails_ref, outgoing, total_ref) = refs
        pairs = total_ref.shape[0]
        unit, radius = normalize(mm(pick_ref[...], fetched_ref[...]) + hot_sum.get()[...])
        low = unit.astype(BF16)
        sides_ref[0:pairs, :] = low
        query_refs = [own.get()] + list(query_refs)
        direction = loss_side(low, query_refs, total_ref, sharp_ref[0], add_ref[0])
        for i, ref in enumerate(query_refs):
            tails_ref[i] = ref[pairs:, :]
        grad = project(unit, radius, direction).astype(BF16)
        sides_ref[pairs:, :] = grad
        place_ref = place.get()
        width = outgoing.width
        outgoing.run(lambda i: mm(place_ref[pl.ds(i * width, width), :], grad).astype(BF16))

    return kernel


def query_side(sharp_ref, add_ref, query, *refs):
    item_refs, (out, total_ref) = refs[:-2], refs[-2:]
    unit, radius = normalize(query.get()[...].astype(F32))
    direction = loss_side(unit.astype(BF16), item_refs, total_ref, sharp_ref[0], add_ref[0])
    out.write(project(unit, radius, direction))
    out.finish()


def hot_terms(blocks, slots):
    def kernel(block_ref, lines_ref, *refs):
        side_refs, (out, total_ref) = refs[:blocks], refs[blocks:]
        width, pairs = total_ref.shape
        row = (iota((width, pairs), 0) + block_ref[0] * width).astype(F32)
        for i, ref in enumerate(side_refs):
            line = lines_ref[i].astype(F32)
            counts = jnp.zeros((width, pairs), F32)
            for h in range(slots):
                counts += (line[h : h + 1, :] * 64.0 + line[h + slots : h + slots + 1, :] == row).astype(F32)
            term = mm(counts.astype(BF16), ref[pairs:, :])
            total_ref[...] = term if i == 0 else total_ref[...] + term
        out.write(total_ref[...].astype(BF16))
        out.finish()

    return kernel


def hot_sum_spread(parts_ref, out):
    piece = jnp.sum(parts_ref[...].astype(F32), axis=0, keepdims=True)
    out.write(jnp.broadcast_to(piece, parts_ref.shape).astype(BF16))
    out.finish()


def widen(blocks):
    def kernel(block_ref, *refs):
        part_refs, out = refs[:blocks], refs[blocks]
        chips = blocks // 2
        width = part_refs[0].shape[0]
        mine, core = block_ref[0] // 2, block_ref[0] % 2
        copies = []
        for i, ref in enumerate(part_refs):
            chip = (mine + chips - i % chips) % chips
            index = chip * 2 + (core if i < chips else 1 - core)
            part = pl.ds(i * width, width)
            out.stage[part, :] = ref[...].astype(F32)
            place = pl.ds(pl.multiple_of(index * width, width), width)
            copies.append(pltpu.make_async_copy(out.stage.at[part], out.out.at[place], out.sem.at[i]))
            copies[-1].start()
        for copy in copies:
            copy.wait()

    return kernel


def cold_terms(same_core):
    def kernel(block_ref, ask_ref, grad_ref, out_ref, row_ref):
        chips, width, _ = out_ref.shape
        total = grad_ref.shape[0]
        owners = ask_ref.shape[0]
        cap = total // owners
        for o in range(owners):
            row_ref[:, o * cap : (o + 1) * cap] = ask_ref[o, 0:1, 0:cap]
        core = block_ref[0] % 2
        core = core if same_core else 1 - core

        def step(i, _):
            chip = (block_ref[0] // 2 + i) % chips
            row = iota((width, total), 0) + (chip * 2 + core) * width
            hit = (row_ref[...] == row).astype(F32).astype(BF16)
            out_ref[i] = mm(hit, grad_ref[...]).astype(out_ref.dtype)
            return 0

        lax.fori_loop(0, chips, step, 0)

    return kernel


def cold_join(mine_ref, theirs_ref, keep_ref, *send_refs):
    keep_ref[...] = mine_ref[0] + theirs_ref[0].astype(F32)
    for d, ref in enumerate(send_refs):
        ref[...] = (mine_ref[d + 1] + theirs_ref[d + 1].astype(F32)).astype(BF16)


def add_parts(keep_ref, *refs):
    part_refs, out = refs[:-1], refs[-1]
    total = keep_ref[...]
    for ref in part_refs:
        total += ref[...].astype(F32)
    out.write(total)
    out.finish()


def swap(array, axis):
    return lax.all_to_all(array, axis, split_axis=0, concat_axis=0, tiled=True)


def cross(array, blocks):
    return lax.ppermute(array, "blk", [(i, i ^ 1) for i in range(blocks)])


def shift(array, blocks, d):
    return lax.ppermute(array, "blk", [(i, (i + 2 * d) % blocks) for i in range(blocks)])


def gather_blocks(array, blocks):
    first = cross(array, blocks)
    mine = [shift(array, blocks, d) for d in range(1, blocks // 2)]
    return [array] + mine + [first] + [cross(m, blocks) for m in mine]


def step_of(queries, hot_table, cold_table, lines, parent, place, tally, sharpness, additive):
    pairs, width = queries.shape
    owners, blocks = lax.axis_size("shard"), lax.axis_size("blk")
    chips = blocks // 2
    slots = parent.shape[1]
    cap = 2 * pairs * slots // owners
    total = owners * cap
    rows = cold_table.shape[0]
    hot_rows = hot_table.shape[0]
    block = lax.axis_index("blk").astype(jnp.int32).reshape(1)

    rank, rank_t, ask, table_low = call(
        make_requests(owners, cap),
        [shape((pairs, LANES), BF16), shape((LANES, pairs), BF16), HBM((owners, 8, LANES), jnp.int32), shape((rows, width), BF16)],
        parent.T, place.T, tally.reshape(1, pairs), cold_table,
        kinds=["h"] * 4,
        scratch=[pltpu.VMEM((1, total), F32)],
        flops=2 * pairs * total * LANES * 3,
    )
    asked = swap(ask, "shard")

    steps = 8
    (looked,) = call(
        fetch,
        [HBM((owners, cap, width), BF16)],
        asked, table_low,
        steps=steps,
        flops=2 * total * rows * width,
    )
    looked, queries, rank, rank_t = lax.optimization_barrier((looked, queries, rank, rank_t))
    fetched = swap(looked, "shard").reshape(total, width)

    lines_t = lines.T
    (query_block,) = call(unit_queries, [shape((pairs + 16, width), BF16)], queries, lines_t, kinds=["h", "h"])
    query_blocks = gather_blocks(query_block, blocks)

    pick, placed, hot_sum = call(
        prepare(cap),
        [shape((pairs, total), BF16), HBM((total, pairs), BF16), HBM((pairs, width), F32)],
        rank, rank_t, lines_t, hot_table,
        kinds=["v", "v", "h", "h"],
        steps=steps,
        flops=2 * pairs * total * (width + 2 * LANES),
    )

    sides, tails, outgoing = call(
        item_side(blocks),
        [shape((2 * pairs, width), BF16), shape((blocks, 16, width), BF16), HBM((total, width), BF16)],
        sharpness, additive, fetched, pick, hot_sum, placed, *query_blocks,
        kinds=["s", "s", "v", "v", "h", "h", "h"] + ["v"] * (blocks - 1),
        scratch=[pltpu.VMEM((pairs, width), F32)],
        steps=steps,
        flops=2 * pairs * width * (2 * total + 2 * blocks * pairs),
    )
    incoming = swap(outgoing.reshape(owners, cap, width), "shard").reshape(total, width)

    side_blocks = gather_blocks(sides, blocks)
    (hot_block,) = call(
        hot_terms(blocks, slots),
        [HBM((hot_rows // blocks, width), BF16)],
        block, tails, *side_blocks,
        kinds=["s"] + ["v"] * (blocks + 1),
        scratch=[pltpu.VMEM((hot_rows // blocks, width), F32)],
        flops=2 * blocks * pairs * width * hot_rows // blocks,
    )
    (query_grad,) = call(
        query_side,
        [HBM((pairs, width), F32)],
        sharpness, additive, queries, *side_blocks,
        kinds=["s", "s", "h"] + ["v"] * blocks,
        scratch=[pltpu.VMEM((pairs, width), F32)],
        flops=4 * pairs * width * blocks * pairs,
    )
    hot_parts = swap(hot_block.reshape(owners, hot_rows // blocks // owners, width), "shard")
    (hot_piece,) = call(hot_sum_spread, [HBM(hot_parts.shape, BF16)], hot_parts)

    def cold_half(same_core, dtype, incoming):
        return call(
            cold_terms(same_core),
            [shape((chips, rows // blocks, width), dtype)],
            block, asked, incoming,
            kinds=["s", "v", "v"],
            scratch=[pltpu.VMEM((1, total), jnp.int32)],
            flops=total * rows * width,
        )[0]

    theirs = cold_half(False, BF16, incoming)
    theirs = cross(theirs, blocks)
    mine = cold_half(True, F32, incoming)
    keep, *sends = call(
        cold_join,
        [shape((rows // blocks, width), F32)] + [shape((rows // blocks, width), BF16)] * (chips - 1),
        mine, theirs,
    )
    hot_block = swap(hot_piece, "shard").reshape(hot_rows // blocks, width)
    parts = [shift(part, blocks, d + 1) for d, part in enumerate(sends)]
    (cold_grad,) = call(add_parts, [HBM((rows // blocks, width), F32)], keep, *parts)
    hot_blocks = gather_blocks(hot_block, blocks)
    (hot_grad,) = call(
        widen(blocks),
        [HBM((hot_rows, width), F32)],
        block, *hot_blocks,
        kinds=["s"] + ["v"] * blocks,
        steps=blocks,
    )
    return (query_grad, hot_grad, cold_grad)


def solution(mesh):
    pair = P(("shard", "blk"), None)
    in_specs = (pair, P(), P("shard", None), pair, pair, pair, P(("shard", "blk")), P(), P())
    return jax.shard_map(step_of, mesh=mesh, in_specs=in_specs, out_specs=(pair, P(), pair), check_vma=False)
```

```python
import jax
import jax.numpy as jnp
from jax import lax
from jax.experimental import pallas as pl
from jax.experimental.pallas import tpu as pltpu
from jax.sharding import PartitionSpec as P


epsilon = 1e-06
F32 = jnp.float32
BF16 = jnp.bfloat16
NN = (((1,), (0,)), ((), ()))
NT = (((1,), (1,)), ((), ()))


def mm(a, b, dims=NN):
    return lax.dot_general(a, b, dims, preferred_element_type=F32)


def iota(shape, dim):
    return lax.broadcasted_iota(jnp.int32, shape, dim)


HBM = pltpu.HBM


class Late:
    def __init__(self, source, buffer, sem):
        self.copy = pltpu.make_async_copy(source, buffer, sem)
        self.buffer = buffer
        self.copy.start()
        self.waits = True

    def get(self):
        if self.waits:
            self.copy.wait()
            self.waits = False
        return self.buffer


class Leave:
    def __init__(self, out_ref, stage_ref, sem):
        self.out, self.stage, self.sem = out_ref, stage_ref, sem
        self.steps = sem.shape[0]
        self.width = stage_ref.shape[0] // self.steps

    def copy(self, i):
        part = pl.ds(i * self.width, self.width)
        return pltpu.make_async_copy(self.stage.at[part], self.out.at[part], self.sem.at[i])

    def write(self, value):
        self.stage[...] = value
        self.start()

    def start(self):
        for i in range(self.steps):
            self.copy(i).start()

    def finish(self):
        for i in range(self.steps):
            self.copy(i).wait()

    def run(self, compute):
        def step(i, _):
            self.stage[pl.ds(i * self.width, self.width)] = compute(i)
            self.copy(i).start()
            return 0

        def finish(i, _):
            self.copy(i).wait()
            return 0

        lax.fori_loop(0, self.steps, step, 0)
        lax.fori_loop(0, self.steps, finish, 0)


def call(kernel, outs, *args, kinds=None, scratch=(), flops=0, steps=1):
    kinds = kinds or ["v"] * len(args)
    late = [k for k, kind in enumerate(kinds) if kind == "h" or isinstance(kind, slice)]
    leaves = [k for k, out in enumerate(outs) if not isinstance(out, jax.ShapeDtypeStruct)]
    operands = [pltpu.with_memory_space_constraint(a, HBM) if k in late else a for k, a in enumerate(args)]
    spaces = [pltpu.SMEM if kind == "s" else HBM if k in late else pltpu.VMEM for k, kind in enumerate(kinds)]
    buffers = []
    for k in late:
        rows = args[k].shape[0] if kinds[k] == "h" else kinds[k].stop - kinds[k].start
        buffers += [pltpu.VMEM((rows,) + args[k].shape[1:], args[k].dtype), pltpu.SemaphoreType.DMA]
    for k in leaves:
        buffers += [pltpu.VMEM(outs[k].shape, outs[k].dtype), pltpu.SemaphoreType.DMA((steps,))]

    def run(*refs):
        refs, extra = list(refs[: len(refs) - len(buffers)]), list(refs[len(refs) - len(buffers) :])
        for k in late:
            source = refs[k] if kinds[k] == "h" else refs[k].at[kinds[k]]
            refs[k] = Late(source, extra.pop(0), extra.pop(0))
        for k in leaves:
            refs[len(args) + k] = Leave(refs[len(args) + k], extra.pop(0), extra.pop(0))
        kernel(*refs)

    moved = sum(a.size * a.dtype.itemsize for a in args)
    return pl.pallas_call(
        run,
        out_shape=list(outs),
        in_specs=[pl.BlockSpec(memory_space=space) for space in spaces],
        out_specs=[pl.BlockSpec(memory_space=HBM if k in leaves else pltpu.VMEM) for k in range(len(outs))],
        scratch_shapes=list(scratch) + buffers,
        compiler_params=pltpu.CompilerParams(vmem_limit_bytes=24 << 20),
        cost_estimate=pl.CostEstimate(flops=flops, bytes_accessed=moved, transcendentals=0),
    )(*operands)


def shape(dims, dtype):
    return jax.ShapeDtypeStruct(dims, dtype)


def expander(owners, cap, base, width):
    return ((iota((owners, width), 1) + base) // cap == iota((owners, width), 0)).astype(F32).astype(BF16)


LANES = 128


def make_requests(owners, cap):
    def kernel(parent, place, tally, rank_ref, rank_t_ref, ask):
        parent_ref, place_ref = parent.get(), place.get()
        slots, pairs = parent_ref.shape
        line = iota((LANES, pairs), 0)
        tally = tally.get()[...]
        named = jnp.zeros((LANES, pairs), F32)
        where = jnp.zeros((LANES, pairs), F32)
        for c in range(slots):
            hit = jnp.logical_and(parent_ref[c : c + 1, :] == line, tally > c)
            named = jnp.where(hit, 1.0, named)
            where = jnp.where(hit, place_ref[c : c + 1, :].astype(F32), where)
        before = (iota((pairs, pairs), 0) < iota((pairs, pairs), 1)).astype(F32).astype(BF16)
        rank_t = jnp.where(named > 0, mm(named.astype(BF16), before), -1.0)
        own_rank, own_place = rank_t[0:owners], where[0:owners]
        lane = iota((owners, LANES), 1)
        asks = jnp.zeros((owners, LANES), F32)
        for p in range(cap):
            row = jnp.sum(jnp.where(own_rank == p, own_place, 0.0), axis=1, keepdims=True)
            asks = jnp.where(lane == p, row, asks)
        asks = asks.astype(jnp.int32)
        for o in range(owners):
            ask.stage[o] = jnp.broadcast_to(asks[o : o + 1, :], ask.stage.shape[1:])
        ask.start()
        rank_t_ref[...] = rank_t.astype(BF16)
        rank_ref[...] = rank_t.T.astype(BF16)
        ask.finish()

    return kernel


def narrow(table, out_ref):
    out_ref[...] = table.get()[...].astype(BF16)


def normalize(rows):
    radius = jnp.sqrt(jnp.sum(rows * rows, axis=1, keepdims=True) + epsilon)
    return rows / radius, radius


def unit_queries(query, lines, send_ref):
    query_ref, lines_ref = query.get(), lines.get()
    pairs = query_ref.shape[0]
    slots = lines_ref.shape[0]
    unit, _ = normalize(query_ref[...].astype(F32))
    send_ref[0:pairs, :] = unit.astype(BF16)
    tail = send_ref.shape[0] - pairs
    line = iota((tail, pairs), 0)
    extra = jnp.zeros((tail, pairs), F32)
    for h in range(slots):
        row = lines_ref[h : h + 1, :]
        extra = jnp.where(line == h, (row // 64).astype(F32), extra)
        extra = jnp.where(line == h + slots, (row % 64).astype(F32), extra)
    send_ref[pairs:, :] = extra.astype(BF16)


def prepare(cap):
    def kernel(rank_ref, rank_t_ref, lines, hot, pick_ref, placed, hot_sum):
        lines_ref = lines.get()
        pairs = rank_ref.shape[0]
        slots = lines_ref.shape[0]
        rank, rank_t = rank_ref[...], rank_t_ref[...]
        line = iota((LANES, pairs), 0)
        lines = jnp.zeros((LANES, pairs), F32)
        for h in range(slots):
            lines = jnp.where(line == h, lines_ref[h : h + 1, :].astype(F32), lines)
        lines = lines.T.astype(jnp.int32)
        width = placed.width
        want = (iota((pairs, width), 1) % cap).astype(F32)
        want_t = (iota((width, pairs), 0) % cap).astype(F32)
        hot_ref = hot.get()
        hot_sum_ref = hot_sum.stage
        hot_sum_ref[...] = jnp.zeros_like(hot_sum_ref)

        def compute(i):
            base = pl.multiple_of(i * width, width)
            spread = expander(LANES, cap, base, width)
            pick_ref[:, pl.ds(base, width)] = (mm(rank, spread) == want).astype(F32).astype(BF16)
            column = iota((pairs, width), 1) + base
            counts = jnp.zeros((pairs, width), F32)
            for h in range(slots):
                counts += (lines[:, h : h + 1] == column).astype(F32)
            hot_sum_ref[...] += mm(counts.astype(BF16), hot_ref[pl.ds(base, width), :])
            spread_t = ((iota((width, LANES), 0) + base) // cap == iota((width, LANES), 1))
            hit = mm(spread_t.astype(F32).astype(BF16), rank_t) == want_t
            return hit.astype(F32).astype(BF16)

        placed.run(compute)
        hot_sum.start()
        hot_sum.finish()

    return kernel


def fetch(ask_ref, table_ref, out, column_ref):
    rows = table_ref.shape[0]
    owners, cap, _ = out.stage.shape
    group = out.width
    diagonal = iota((cap, cap), 0) == iota((cap, cap), 1)
    for o in range(owners):
        ask = ask_ref[o, 0:1, 0:cap].astype(F32)
        column_ref[o * cap : (o + 1) * cap, :] = jnp.sum(
            jnp.where(diagonal, ask, 0.0), axis=1, keepdims=True
        ).astype(jnp.int32)
    size = group * cap
    lane = iota((size, rows), 1).astype(jnp.int16)

    def compute(i):
        column = column_ref[pl.ds(i * size, size), :]
        column = jnp.broadcast_to(column, (size, LANES)).astype(jnp.int16)
        column = jnp.tile(column, (1, rows // LANES))
        hit = jnp.where(column == lane, jnp.ones((), BF16), jnp.zeros((), BF16))
        return mm(hit, table_ref[...]).astype(BF16).reshape(group, cap, table_ref.shape[1])

    out.run(compute)


def loss_side(own_low, other_refs, total_ref, sharpness, additive):
    rows = own_low.shape[0]
    for i, ref in enumerate(other_refs):
        other = ref[0:rows, :]
        grad = jax.nn.sigmoid(sharpness * mm(own_low, other, NT) + additive)
        if i == 0:
            grad = grad - (iota((rows, rows), 0) == iota((rows, rows), 1)).astype(F32)
            total_ref[...] = mm(grad.astype(BF16), other)
        else:
            total_ref[...] += mm(grad.astype(BF16), other)
    return sharpness * total_ref[...]


def project(unit, radius, direction):
    inner = jnp.sum(unit * direction, axis=1, keepdims=True)
    return (direction - unit * inner) / radius


def item_side(blocks):
    def kernel(sharp_ref, add_ref, fetched_ref, pick_ref, hot_sum, place, own, *refs):
        query_refs, refs = refs[: blocks - 1], refs[blocks - 1 :]
        (sides_ref, tails_ref, outgoing, total_ref) = refs
        pairs = total_ref.shape[0]
        unit, radius = normalize(mm(pick_ref[...], fetched_ref[...]) + hot_sum.get()[...])
        low = unit.astype(BF16)
        sides_ref[0:pairs, :] = low
        query_refs = [own.get()] + list(query_refs)
        direction = loss_side(low, query_refs, total_ref, sharp_ref[0], add_ref[0])
        for i, ref in enumerate(query_refs):
            tails_ref[i] = ref[pairs:, :]
        grad = project(unit, radius, direction).astype(BF16)
        sides_ref[pairs:, :] = grad
        place_ref = place.get()
        width = outgoing.width
        outgoing.run(lambda i: mm(place_ref[pl.ds(i * width, width), :], grad).astype(BF16))

    return kernel


def query_side(sharp_ref, add_ref, query, *refs):
    item_refs, (out, total_ref) = refs[:-2], refs[-2:]
    unit, radius = normalize(query.get()[...].astype(F32))
    direction = loss_side(unit.astype(BF16), item_refs, total_ref, sharp_ref[0], add_ref[0])
    out.write(project(unit, radius, direction))
    out.finish()


def hot_terms(blocks, slots):
    def kernel(block_ref, lines_ref, *refs):
        side_refs, (out, total_ref) = refs[:blocks], refs[blocks:]
        width, pairs = total_ref.shape
        row = (iota((width, pairs), 0) + block_ref[0] * width).astype(F32)
        for i, ref in enumerate(side_refs):
            line = lines_ref[i].astype(F32)
            counts = jnp.zeros((width, pairs), F32)
            for h in range(slots):
                counts += (line[h : h + 1, :] * 64.0 + line[h + slots : h + slots + 1, :] == row).astype(F32)
            term = mm(counts.astype(BF16), ref[pairs:, :])
            total_ref[...] = term if i == 0 else total_ref[...] + term
        out.write(total_ref[...].astype(BF16))
        out.finish()

    return kernel


def hot_sum_spread(parts_ref, out):
    piece = jnp.sum(parts_ref[...].astype(F32), axis=0, keepdims=True)
    out.write(jnp.broadcast_to(piece, parts_ref.shape).astype(BF16))
    out.finish()


def widen(blocks):
    def kernel(block_ref, *refs):
        part_refs, out = refs[:blocks], refs[blocks]
        chips = blocks // 2
        width = part_refs[0].shape[0]
        mine, core = block_ref[0] // 2, block_ref[0] % 2
        copies = []
        for i, ref in enumerate(part_refs):
            chip = (mine + chips - i % chips) % chips
            index = chip * 2 + (core if i < chips else 1 - core)
            part = pl.ds(i * width, width)
            out.stage[part, :] = ref[...].astype(F32)
            place = pl.ds(pl.multiple_of(index * width, width), width)
            copies.append(pltpu.make_async_copy(out.stage.at[part], out.out.at[place], out.sem.at[i]))
            copies[-1].start()
        for copy in copies:
            copy.wait()

    return kernel


def cold_terms(same_core):
    def kernel(block_ref, ask_ref, grad_ref, out_ref, row_ref):
        chips, width, _ = out_ref.shape
        total = grad_ref.shape[0]
        owners = ask_ref.shape[0]
        cap = total // owners
        for o in range(owners):
            row_ref[:, o * cap : (o + 1) * cap] = ask_ref[o, 0:1, 0:cap]
        core = block_ref[0] % 2
        core = core if same_core else 1 - core

        def step(i, _):
            chip = (block_ref[0] // 2 + i) % chips
            row = iota((width, total), 0) + (chip * 2 + core) * width
            hit = (row_ref[...] == row).astype(F32).astype(BF16)
            out_ref[i] = mm(hit, grad_ref[...]).astype(out_ref.dtype)
            return 0

        lax.fori_loop(0, chips, step, 0)

    return kernel


def cold_join(mine_ref, theirs_ref, keep_ref, *send_refs):
    keep_ref[...] = mine_ref[0] + theirs_ref[0].astype(F32)
    for d, ref in enumerate(send_refs):
        ref[...] = (mine_ref[d + 1] + theirs_ref[d + 1].astype(F32)).astype(BF16)


def add_parts(keep_ref, *refs):
    part_refs, out = refs[:-1], refs[-1]
    total = keep_ref[...]
    for ref in part_refs:
        total += ref[...].astype(F32)
    out.write(total)
    out.finish()


def swap(array, axis):
    return lax.all_to_all(array, axis, split_axis=0, concat_axis=0, tiled=True)


def cross(array, blocks):
    return lax.ppermute(array, "blk", [(i, i ^ 1) for i in range(blocks)])


def shift(array, blocks, d):
    return lax.ppermute(array, "blk", [(i, (i + 2 * d) % blocks) for i in range(blocks)])


def gather_blocks(array, blocks):
    first = cross(array, blocks)
    mine = [shift(array, blocks, d) for d in range(1, blocks // 2)]
    return [array] + mine + [first] + [cross(m, blocks) for m in mine]


def step_of(queries, hot_table, cold_table, lines, parent, place, tally, sharpness, additive):
    pairs, width = queries.shape
    owners, blocks = lax.axis_size("shard"), lax.axis_size("blk")
    chips = blocks // 2
    slots = parent.shape[1]
    cap = 2 * pairs * slots // owners
    total = owners * cap
    rows = cold_table.shape[0]
    hot_rows = hot_table.shape[0]
    block = lax.axis_index("blk").astype(jnp.int32).reshape(1)

    rank, rank_t, ask = call(
        make_requests(owners, cap),
        [shape((pairs, LANES), BF16), shape((LANES, pairs), BF16), HBM((owners, 8, LANES), jnp.int32)],
        parent.T, place.T, tally.reshape(1, pairs),
        kinds=["h"] * 3,
        flops=2 * pairs * pairs * LANES,
    )
    (table_low,) = call(narrow, [shape((rows, width), BF16)], cold_table, kinds=["h"])
    asked = swap(ask, "shard")

    steps = 8
    (looked,) = call(
        fetch,
        [HBM((owners, cap, width), BF16)],
        asked, table_low,
        scratch=[pltpu.VMEM((total, 1), jnp.int32)],
        steps=steps,
        flops=2 * total * rows * width,
    )
    looked, queries, rank, rank_t = lax.optimization_barrier((looked, queries, rank, rank_t))
    fetched = swap(looked, "shard").reshape(total, width)

    lines_t = lines.T
    (query_block,) = call(unit_queries, [shape((pairs + 16, width), BF16)], queries, lines_t, kinds=["h", "h"])
    query_blocks = gather_blocks(query_block, blocks)

    pick, placed, hot_sum = call(
        prepare(cap),
        [shape((pairs, total), BF16), HBM((total, pairs), BF16), HBM((pairs, width), F32)],
        rank, rank_t, lines_t, hot_table,
        kinds=["v", "v", "h", "h"],
        steps=steps,
        flops=2 * pairs * total * (width + 2 * LANES),
    )

    sides, tails, outgoing = call(
        item_side(blocks),
        [shape((2 * pairs, width), BF16), shape((blocks, 16, width), BF16), HBM((total, width), BF16)],
        sharpness, additive, fetched, pick, hot_sum, placed, *query_blocks,
        kinds=["s", "s", "v", "v", "h", "h", "h"] + ["v"] * (blocks - 1),
        scratch=[pltpu.VMEM((pairs, width), F32)],
        steps=steps,
        flops=2 * pairs * width * (2 * total + 2 * blocks * pairs),
    )
    incoming = swap(outgoing.reshape(owners, cap, width), "shard").reshape(total, width)

    side_blocks = gather_blocks(sides, blocks)
    (hot_block,) = call(
        hot_terms(blocks, slots),
        [HBM((hot_rows // blocks, width), BF16)],
        block, tails, *side_blocks,
        kinds=["s"] + ["v"] * (blocks + 1),
        scratch=[pltpu.VMEM((hot_rows // blocks, width), F32)],
        flops=2 * blocks * pairs * width * hot_rows // blocks,
    )
    (query_grad,) = call(
        query_side,
        [HBM((pairs, width), F32)],
        sharpness, additive, queries, *side_blocks,
        kinds=["s", "s", "h"] + ["v"] * blocks,
        scratch=[pltpu.VMEM((pairs, width), F32)],
        flops=4 * pairs * width * blocks * pairs,
    )
    hot_parts = swap(hot_block.reshape(owners, hot_rows // blocks // owners, width), "shard")
    (hot_piece,) = call(hot_sum_spread, [HBM(hot_parts.shape, BF16)], hot_parts)

    def cold_half(same_core, dtype, incoming):
        return call(
            cold_terms(same_core),
            [shape((chips, rows // blocks, width), dtype)],
            block, asked, incoming,
            kinds=["s", "v", "v"],
            scratch=[pltpu.VMEM((1, total), jnp.int32)],
            flops=total * rows * width,
        )[0]

    theirs = cold_half(False, BF16, incoming)
    theirs = cross(theirs, blocks)
    mine = cold_half(True, F32, incoming)
    keep, *sends = call(
        cold_join,
        [shape((rows // blocks, width), F32)] + [shape((rows // blocks, width), BF16)] * (chips - 1),
        mine, theirs,
    )
    hot_block = swap(hot_piece, "shard").reshape(hot_rows // blocks, width)
    parts = [shift(part, blocks, d + 1) for d, part in enumerate(sends)]
    (cold_grad,) = call(add_parts, [HBM((rows // blocks, width), F32)], keep, *parts)
    hot_blocks = gather_blocks(hot_block, blocks)
    (hot_grad,) = call(
        widen(blocks),
        [HBM((hot_rows, width), F32)],
        block, *hot_blocks,
        kinds=["s"] + ["v"] * blocks,
        steps=blocks,
    )
    return (query_grad, hot_grad, cold_grad)


def solution(mesh):
    pair = P(("shard", "blk"), None)
    in_specs = (pair, P(), P("shard", None), pair, pair, pair, P(("shard", "blk")), P(), P())
    return jax.shard_map(step_of, mesh=mesh, in_specs=in_specs, out_specs=(pair, P(), pair), check_vma=False)
```

```python
import jax
import jax.numpy as jnp
from jax import lax
from jax.experimental import pallas as pl
from jax.experimental.pallas import tpu as pltpu
from jax.sharding import PartitionSpec as P


epsilon = 1e-06
F32 = jnp.float32
BF16 = jnp.bfloat16
NN = (((1,), (0,)), ((), ()))
NT = (((1,), (1,)), ((), ()))


def mm(a, b, dims=NN):
    return lax.dot_general(a, b, dims, preferred_element_type=F32)


def iota(shape, dim):
    return lax.broadcasted_iota(jnp.int32, shape, dim)


HBM = pltpu.HBM


class Late:
    def __init__(self, source, buffer, sem):
        self.copy = pltpu.make_async_copy(source, buffer, sem)
        self.buffer = buffer
        self.copy.start()
        self.waits = True

    def get(self):
        if self.waits:
            self.copy.wait()
            self.waits = False
        return self.buffer


class Leave:
    def __init__(self, out_ref, stage_ref, sem):
        self.out, self.stage, self.sem = out_ref, stage_ref, sem
        self.steps = sem.shape[0]
        self.width = stage_ref.shape[0] // self.steps

    def copy(self, i):
        part = pl.ds(i * self.width, self.width)
        return pltpu.make_async_copy(self.stage.at[part], self.out.at[part], self.sem.at[i])

    def write(self, value):
        self.stage[...] = value
        self.start()

    def start(self):
        for i in range(self.steps):
            self.copy(i).start()

    def finish(self):
        for i in range(self.steps):
            self.copy(i).wait()

    def run(self, compute):
        def step(i, _):
            self.stage[pl.ds(i * self.width, self.width)] = compute(i)
            self.copy(i).start()
            return 0

        def finish(i, _):
            self.copy(i).wait()
            return 0

        lax.fori_loop(0, self.steps, step, 0)
        lax.fori_loop(0, self.steps, finish, 0)


def call(kernel, outs, *args, kinds=None, scratch=(), flops=0, steps=1):
    kinds = kinds or ["v"] * len(args)
    late = [k for k, kind in enumerate(kinds) if kind == "h" or isinstance(kind, slice)]
    leaves = [k for k, out in enumerate(outs) if not isinstance(out, jax.ShapeDtypeStruct)]
    operands = [pltpu.with_memory_space_constraint(a, HBM) if k in late else a for k, a in enumerate(args)]
    spaces = [pltpu.SMEM if kind == "s" else HBM if k in late else pltpu.VMEM for k, kind in enumerate(kinds)]
    buffers = []
    for k in late:
        rows = args[k].shape[0] if kinds[k] == "h" else kinds[k].stop - kinds[k].start
        buffers += [pltpu.VMEM((rows,) + args[k].shape[1:], args[k].dtype), pltpu.SemaphoreType.DMA]
    for k in leaves:
        buffers += [pltpu.VMEM(outs[k].shape, outs[k].dtype), pltpu.SemaphoreType.DMA((steps,))]

    def run(*refs):
        refs, extra = list(refs[: len(refs) - len(buffers)]), list(refs[len(refs) - len(buffers) :])
        for k in late:
            source = refs[k] if kinds[k] == "h" else refs[k].at[kinds[k]]
            refs[k] = Late(source, extra.pop(0), extra.pop(0))
        for k in leaves:
            refs[len(args) + k] = Leave(refs[len(args) + k], extra.pop(0), extra.pop(0))
        kernel(*refs)

    moved = sum(a.size * a.dtype.itemsize for a in args)
    return pl.pallas_call(
        run,
        out_shape=list(outs),
        in_specs=[pl.BlockSpec(memory_space=space) for space in spaces],
        out_specs=[pl.BlockSpec(memory_space=HBM if k in leaves else pltpu.VMEM) for k in range(len(outs))],
        scratch_shapes=list(scratch) + buffers,
        compiler_params=pltpu.CompilerParams(vmem_limit_bytes=24 << 20),
        cost_estimate=pl.CostEstimate(flops=flops, bytes_accessed=moved, transcendentals=0),
    )(*operands)


def shape(dims, dtype):
    return jax.ShapeDtypeStruct(dims, dtype)


def expander(owners, cap, base, width):
    return ((iota((owners, width), 1) + base) // cap == iota((owners, width), 0)).astype(F32).astype(BF16)


LANES = 128


def make_requests(owners, cap):
    def kernel(parent, place, tally, rank_ref, rank_t_ref, ask):
        parent_ref, place_ref = parent.get(), place.get()
        slots, pairs = parent_ref.shape
        line = iota((LANES, pairs), 0)
        tally = tally.get()[...]
        named = jnp.zeros((LANES, pairs), F32)
        where = jnp.zeros((LANES, pairs), F32)
        for c in range(slots):
            hit = jnp.logical_and(parent_ref[c : c + 1, :] == line, tally > c)
            named = jnp.where(hit, 1.0, named)
            where = jnp.where(hit, place_ref[c : c + 1, :].astype(F32), where)
        before = (iota((pairs, pairs), 0) < iota((pairs, pairs), 1)).astype(F32).astype(BF16)
        rank_t = jnp.where(named > 0, mm(named.astype(BF16), before), -1.0)
        own_rank, own_place = rank_t[0:owners], where[0:owners]
        lane = iota((owners, LANES), 1)
        asks = jnp.zeros((owners, LANES), F32)
        for p in range(cap):
            row = jnp.sum(jnp.where(own_rank == p, own_place, 0.0), axis=1, keepdims=True)
            asks = jnp.where(lane == p, row, asks)
        asks = asks.astype(jnp.int32)
        for o in range(owners):
            ask.stage[o] = jnp.broadcast_to(asks[o : o + 1, :], ask.stage.shape[1:])
        ask.start()
        rank_t_ref[...] = rank_t.astype(BF16)
        rank_ref[...] = rank_t.T.astype(BF16)
        ask.finish()

    return kernel


def narrow(table, out_ref):
    out_ref[...] = table.get()[...].astype(BF16)


def normalize(rows):
    radius = jnp.sqrt(jnp.sum(rows * rows, axis=1, keepdims=True) + epsilon)
    return rows / radius, radius


def unit_queries(query, lines, send_ref):
    query_ref, lines_ref = query.get(), lines.get()
    pairs = query_ref.shape[0]
    slots = lines_ref.shape[0]
    unit, _ = normalize(query_ref[...].astype(F32))
    send_ref[0:pairs, :] = unit.astype(BF16)
    tail = send_ref.shape[0] - pairs
    line = iota((tail, pairs), 0)
    extra = jnp.zeros((tail, pairs), F32)
    for h in range(slots):
        row = lines_ref[h : h + 1, :]
        extra = jnp.where(line == h, (row // 64).astype(F32), extra)
        extra = jnp.where(line == h + slots, (row % 64).astype(F32), extra)
    send_ref[pairs:, :] = extra.astype(BF16)


def prepare(cap):
    def kernel(rank_ref, rank_t_ref, lines, hot, pick_ref, placed, hot_sum_ref):
        lines_ref = lines.get()
        pairs = rank_ref.shape[0]
        slots = lines_ref.shape[0]
        rank, rank_t = rank_ref[...], rank_t_ref[...]
        line = iota((LANES, pairs), 0)
        lines = jnp.zeros((LANES, pairs), F32)
        for h in range(slots):
            lines = jnp.where(line == h, lines_ref[h : h + 1, :].astype(F32), lines)
        lines = lines.T.astype(jnp.int32)
        width = placed.width
        want = (iota((pairs, width), 1) % cap).astype(F32)
        want_t = (iota((width, pairs), 0) % cap).astype(F32)
        hot_ref = hot.get()
        hot_sum_ref[...] = jnp.zeros_like(hot_sum_ref)

        def compute(i):
            base = pl.multiple_of(i * width, width)
            spread = expander(LANES, cap, base, width)
            pick_ref[:, pl.ds(base, width)] = (mm(rank, spread) == want).astype(F32).astype(BF16)
            column = iota((pairs, width), 1) + base
            counts = jnp.zeros((pairs, width), F32)
            for h in range(slots):
                counts += (lines[:, h : h + 1] == column).astype(F32)
            hot_sum_ref[...] += mm(counts.astype(BF16), hot_ref[pl.ds(base, width), :])
            spread_t = ((iota((width, LANES), 0) + base) // cap == iota((width, LANES), 1))
            hit = mm(spread_t.astype(F32).astype(BF16), rank_t) == want_t
            return hit.astype(F32).astype(BF16)

        placed.run(compute)

    return kernel


def fetch(ask_ref, table_ref, out, column_ref):
    rows = table_ref.shape[0]
    owners, cap, _ = out.stage.shape
    group = out.width
    diagonal = iota((cap, cap), 0) == iota((cap, cap), 1)
    for o in range(owners):
        ask = ask_ref[o, 0:1, 0:cap].astype(F32)
        column_ref[o * cap : (o + 1) * cap, :] = jnp.sum(
            jnp.where(diagonal, ask, 0.0), axis=1, keepdims=True
        ).astype(jnp.int32)
    size = group * cap
    lane = iota((size, rows), 1).astype(jnp.int16)

    def compute(i):
        column = column_ref[pl.ds(i * size, size), :]
        column = jnp.broadcast_to(column, (size, LANES)).astype(jnp.int16)
        column = jnp.tile(column, (1, rows // LANES))
        hit = jnp.where(column == lane, jnp.ones((), BF16), jnp.zeros((), BF16))
        return mm(hit, table_ref[...]).astype(BF16).reshape(group, cap, table_ref.shape[1])

    out.run(compute)


def loss_side(own_low, others, own_at, sharpness, additive):
    rows = own_low.shape[0]
    others = [other[0:rows, :] for other in others]
    grads = []
    for i, other in enumerate(others):
        grad = jax.nn.sigmoid(sharpness * mm(own_low, other, NT) + additive)
        if i == own_at:
            grad = grad - (iota((rows, rows), 0) == iota((rows, rows), 1)).astype(F32)
        grads.append(grad.astype(BF16))
    return sharpness * mm(jnp.concatenate(grads, axis=1), jnp.concatenate(others, axis=0))


def project(unit, radius, direction):
    inner = jnp.sum(unit * direction, axis=1, keepdims=True)
    return (direction - unit * inner) / radius


def item_side(near, far):
    def kernel(sharp_ref, add_ref, fetched_ref, pick_ref, hot_sum_ref, *refs):
        near_refs, far_blocks, place = refs[:near], refs[near : near + far], refs[near + far]
        sides_ref, tails_ref, outgoing = refs[near + far + 1 :]
        pairs = hot_sum_ref.shape[0]
        unit, radius = normalize(mm(pick_ref[...], fetched_ref[...]) + hot_sum_ref[...])
        low = unit.astype(BF16)
        sides_ref[0:pairs, :] = low
        queries = list(near_refs) + [block.get() for block in far_blocks]
        for i, ref in enumerate(queries):
            tails_ref[i] = ref[pairs:, :]
        direction = loss_side(low, queries, near + far - 1, sharp_ref[0], add_ref[0])
        grad = project(unit, radius, direction).astype(BF16)
        sides_ref[pairs:, :] = grad
        place_ref = place.get()
        width = outgoing.width
        outgoing.run(lambda i: mm(place_ref[pl.ds(i * width, width), :], grad).astype(BF16))

    return kernel


def query_side(sharp_ref, add_ref, query, *refs):
    item_refs, out = refs[:-1], refs[-1]
    unit, radius = normalize(query.get()[...].astype(F32))
    direction = loss_side(unit.astype(BF16), item_refs, 0, sharp_ref[0], add_ref[0])
    out.write(project(unit, radius, direction))
    out.finish()


def hot_terms(blocks, slots):
    def kernel(block_ref, lines_ref, *refs):
        side_refs, (out, total_ref) = refs[:blocks], refs[blocks:]
        width, pairs = total_ref.shape
        row = (iota((width, pairs), 0) + block_ref[0] * width).astype(F32)
        for i, ref in enumerate(side_refs):
            line = lines_ref[i].astype(F32)
            counts = jnp.zeros((width, pairs), F32)
            for h in range(slots):
                counts += (line[h : h + 1, :] * 64.0 + line[h + slots : h + slots + 1, :] == row).astype(F32)
            term = mm(counts.astype(BF16), ref[pairs:, :])
            total_ref[...] = term if i == 0 else total_ref[...] + term
        out.write(total_ref[...].astype(BF16))
        out.finish()

    return kernel


def hot_sum_spread(parts_ref, out):
    piece = jnp.sum(parts_ref[...].astype(F32), axis=0, keepdims=True)
    out.write(jnp.broadcast_to(piece, parts_ref.shape).astype(BF16))
    out.finish()


def widen(blocks):
    def kernel(block_ref, *refs):
        part_refs, out = refs[:blocks], refs[blocks]
        chips = blocks // 2
        width = part_refs[0].shape[0]
        mine, core = block_ref[0] // 2, block_ref[0] % 2
        copies = []
        for i, ref in enumerate(part_refs):
            chip = (mine + chips - i % chips) % chips
            index = chip * 2 + (core if i < chips else 1 - core)
            part = pl.ds(i * width, width)
            out.stage[part, :] = ref[...].astype(F32)
            place = pl.ds(pl.multiple_of(index * width, width), width)
            copies.append(pltpu.make_async_copy(out.stage.at[part], out.out.at[place], out.sem.at[i]))
            copies[-1].start()
        for copy in copies:
            copy.wait()

    return kernel


def cold_terms(same_core):
    def kernel(block_ref, ask_ref, grad_ref, out_ref, row_ref):
        chips, width, _ = out_ref.shape
        total = grad_ref.shape[0]
        owners = ask_ref.shape[0]
        cap = total // owners
        for o in range(owners):
            row_ref[:, o * cap : (o + 1) * cap] = ask_ref[o, 0:1, 0:cap]
        core = block_ref[0] % 2
        core = core if same_core else 1 - core

        def step(i, _):
            chip = (block_ref[0] // 2 + i) % chips
            row = iota((width, total), 0) + (chip * 2 + core) * width
            hit = (row_ref[...] == row).astype(F32).astype(BF16)
            out_ref[i] = mm(hit, grad_ref[...]).astype(out_ref.dtype)
            return 0

        lax.fori_loop(0, chips, step, 0)

    return kernel


def cold_join(mine_ref, theirs_ref, keep_ref, *send_refs):
    keep_ref[...] = mine_ref[0] + theirs_ref[0].astype(F32)
    for d, ref in enumerate(send_refs):
        ref[...] = (mine_ref[d + 1] + theirs_ref[d + 1].astype(F32)).astype(BF16)


def add_parts(keep_ref, *refs):
    part_refs, out = refs[:-1], refs[-1]
    total = keep_ref[...]
    for ref in part_refs:
        total += ref[...].astype(F32)
    out.write(total)
    out.finish()


def swap(array, axis):
    return lax.all_to_all(array, axis, split_axis=0, concat_axis=0, tiled=True)


def cross(array, blocks):
    return lax.ppermute(array, "blk", [(i, i ^ 1) for i in range(blocks)])


def shift(array, blocks, d):
    return lax.ppermute(array, "blk", [(i, (i + 2 * d) % blocks) for i in range(blocks)])


def gather_blocks(array, blocks):
    first = cross(array, blocks)
    mine = [shift(array, blocks, d) for d in range(1, blocks // 2)]
    return [array] + mine + [first] + [cross(m, blocks) for m in mine]


def step_of(queries, hot_table, cold_table, lines, parent, place, tally, sharpness, additive):
    pairs, width = queries.shape
    owners, blocks = lax.axis_size("shard"), lax.axis_size("blk")
    chips = blocks // 2
    slots = parent.shape[1]
    cap = 2 * pairs * slots // owners
    total = owners * cap
    rows = cold_table.shape[0]
    hot_rows = hot_table.shape[0]
    block = lax.axis_index("blk").astype(jnp.int32).reshape(1)

    rank, rank_t, ask = call(
        make_requests(owners, cap),
        [shape((pairs, LANES), BF16), shape((LANES, pairs), BF16), HBM((owners, 8, LANES), jnp.int32)],
        parent.T, place.T, tally.reshape(1, pairs),
        kinds=["h"] * 3,
        flops=2 * pairs * pairs * LANES,
    )
    (table_low,) = call(narrow, [shape((rows, width), BF16)], cold_table, kinds=["h"])
    asked = swap(ask, "shard")

    steps = 8
    (looked,) = call(
        fetch,
        [HBM((owners, cap, width), BF16)],
        asked, table_low,
        scratch=[pltpu.VMEM((total, 1), jnp.int32)],
        steps=steps,
        flops=2 * total * rows * width,
    )
    looked, queries, rank, rank_t = lax.optimization_barrier((looked, queries, rank, rank_t))
    fetched = swap(looked, "shard").reshape(total, width)

    lines_t = lines.T
    (query_block,) = call(unit_queries, [shape((pairs + 16, width), BF16)], queries, lines_t, kinds=["h", "h"])
    query_blocks = gather_blocks(query_block, blocks)

    pick, placed, hot_sum = call(
        prepare(cap),
        [shape((pairs, total), BF16), HBM((total, pairs), BF16), shape((pairs, width), F32)],
        rank, rank_t, lines_t, hot_table,
        kinds=["v", "v", "h", "h"],
        steps=steps,
        flops=2 * pairs * total * (width + 2 * LANES),
    )

    far = 3
    order = list(range(1, blocks)) + [0]
    sides, tails, outgoing = call(
        item_side(blocks - far, far),
        [shape((2 * pairs, width), BF16), shape((blocks, 16, width), BF16), HBM((total, width), BF16)],
        sharpness, additive, fetched, pick, hot_sum, *[query_blocks[i] for i in order], placed,
        kinds=["s", "s", "v", "v", "v"] + ["v"] * (blocks - far) + ["h"] * (far + 1),
        steps=steps,
        flops=2 * pairs * width * (2 * total + 2 * blocks * pairs),
    )
    incoming = swap(outgoing.reshape(owners, cap, width), "shard").reshape(total, width)

    side_blocks = gather_blocks(sides, blocks)
    (hot_block,) = call(
        hot_terms(blocks, slots),
        [HBM((hot_rows // blocks, width), BF16)],
        block, tails, *[side_blocks[i] for i in order],
        kinds=["s"] + ["v"] * (blocks + 1),
        scratch=[pltpu.VMEM((hot_rows // blocks, width), F32)],
        flops=2 * blocks * pairs * width * hot_rows // blocks,
    )
    (query_grad,) = call(
        query_side,
        [HBM((pairs, width), F32)],
        sharpness, additive, queries, *side_blocks,
        kinds=["s", "s", "h"] + ["v"] * blocks,
        flops=4 * pairs * width * blocks * pairs,
    )
    hot_parts = swap(hot_block.reshape(owners, hot_rows // blocks // owners, width), "shard")
    (hot_piece,) = call(hot_sum_spread, [HBM(hot_parts.shape, BF16)], hot_parts)

    def cold_half(same_core, dtype, incoming):
        return call(
            cold_terms(same_core),
            [shape((chips, rows // blocks, width), dtype)],
            block, asked, incoming,
            kinds=["s", "v", "v"],
            scratch=[pltpu.VMEM((1, total), jnp.int32)],
            flops=total * rows * width,
        )[0]

    theirs = cold_half(False, BF16, incoming)
    theirs = cross(theirs, blocks)
    mine = cold_half(True, F32, incoming)
    keep, *sends = call(
        cold_join,
        [shape((rows // blocks, width), F32)] + [shape((rows // blocks, width), BF16)] * (chips - 1),
        mine, theirs,
    )
    hot_block = swap(hot_piece, "shard").reshape(hot_rows // blocks, width)
    parts = [shift(part, blocks, d + 1) for d, part in enumerate(sends)]
    (cold_grad,) = call(add_parts, [HBM((rows // blocks, width), F32)], keep, *parts)
    hot_blocks = gather_blocks(hot_block, blocks)
    (hot_grad,) = call(
        widen(blocks),
        [HBM((hot_rows, width), F32)],
        block, *hot_blocks,
        kinds=["s"] + ["v"] * blocks,
        steps=blocks,
    )
    return (query_grad, hot_grad, cold_grad)


def solution(mesh):
    pair = P(("shard", "blk"), None)
    in_specs = (pair, P(), P("shard", None), pair, pair, pair, P(("shard", "blk")), P(), P())
    return jax.shard_map(step_of, mesh=mesh, in_specs=in_specs, out_specs=(pair, P(), pair), check_vma=False)
```

```python
import jax
import jax.numpy as jnp
from jax import lax
from jax.experimental import pallas as pl
from jax.experimental.pallas import tpu as pltpu
from jax.sharding import PartitionSpec as P


epsilon = 1e-06
F32 = jnp.float32
BF16 = jnp.bfloat16
NN = (((1,), (0,)), ((), ()))
NT = (((1,), (1,)), ((), ()))


def mm(a, b, dims=NN):
    return lax.dot_general(a, b, dims, preferred_element_type=F32)


def iota(shape, dim):
    return lax.broadcasted_iota(jnp.int32, shape, dim)


HBM = pltpu.HBM


class Late:
    def __init__(self, source, buffer, sem):
        self.copy = pltpu.make_async_copy(source, buffer, sem)
        self.buffer = buffer
        self.copy.start()
        self.waits = True

    def get(self):
        if self.waits:
            self.copy.wait()
            self.waits = False
        return self.buffer


class Leave:
    def __init__(self, out_ref, stage_ref, sem):
        self.out, self.stage, self.sem = out_ref, stage_ref, sem
        self.steps = sem.shape[0]
        self.width = stage_ref.shape[0] // self.steps

    def copy(self, i):
        part = pl.ds(i * self.width, self.width)
        return pltpu.make_async_copy(self.stage.at[part], self.out.at[part], self.sem.at[i])

    def write(self, value):
        self.stage[...] = value
        self.start()

    def start(self):
        for i in range(self.steps):
            self.copy(i).start()

    def finish(self):
        for i in range(self.steps):
            self.copy(i).wait()

    def run(self, compute):
        def step(i, _):
            self.stage[pl.ds(i * self.width, self.width)] = compute(i)
            self.copy(i).start()
            return 0

        def finish(i, _):
            self.copy(i).wait()
            return 0

        lax.fori_loop(0, self.steps, step, 0)
        lax.fori_loop(0, self.steps, finish, 0)


def call(kernel, outs, *args, kinds=None, scratch=(), flops=0, steps=1):
    kinds = kinds or ["v"] * len(args)
    late = [k for k, kind in enumerate(kinds) if kind == "h" or isinstance(kind, slice)]
    leaves = [k for k, out in enumerate(outs) if not isinstance(out, jax.ShapeDtypeStruct)]
    operands = [pltpu.with_memory_space_constraint(a, HBM) if k in late else a for k, a in enumerate(args)]
    spaces = [pltpu.SMEM if kind == "s" else HBM if k in late else pltpu.VMEM for k, kind in enumerate(kinds)]
    buffers = []
    for k in late:
        rows = args[k].shape[0] if kinds[k] == "h" else kinds[k].stop - kinds[k].start
        buffers += [pltpu.VMEM((rows,) + args[k].shape[1:], args[k].dtype), pltpu.SemaphoreType.DMA]
    for k in leaves:
        buffers += [pltpu.VMEM(outs[k].shape, outs[k].dtype), pltpu.SemaphoreType.DMA((steps,))]

    def run(*refs):
        refs, extra = list(refs[: len(refs) - len(buffers)]), list(refs[len(refs) - len(buffers) :])
        for k in late:
            source = refs[k] if kinds[k] == "h" else refs[k].at[kinds[k]]
            refs[k] = Late(source, extra.pop(0), extra.pop(0))
        for k in leaves:
            refs[len(args) + k] = Leave(refs[len(args) + k], extra.pop(0), extra.pop(0))
        kernel(*refs)

    moved = sum(a.size * a.dtype.itemsize for a in args)
    return pl.pallas_call(
        run,
        out_shape=list(outs),
        in_specs=[pl.BlockSpec(memory_space=space) for space in spaces],
        out_specs=[pl.BlockSpec(memory_space=HBM if k in leaves else pltpu.VMEM) for k in range(len(outs))],
        scratch_shapes=list(scratch) + buffers,
        compiler_params=pltpu.CompilerParams(vmem_limit_bytes=24 << 20),
        cost_estimate=pl.CostEstimate(flops=flops, bytes_accessed=moved, transcendentals=0),
    )(*operands)


def shape(dims, dtype):
    return jax.ShapeDtypeStruct(dims, dtype)


def expander(owners, cap, base, width):
    return ((iota((owners, width), 1) + base) // cap == iota((owners, width), 0)).astype(F32).astype(BF16)


LANES = 128


def make_requests(owners, cap):
    def kernel(parent, place, tally, rank_ref, rank_t_ref, ask):
        parent_ref, place_ref = parent.get(), place.get()
        slots, pairs = parent_ref.shape
        line = iota((LANES, pairs), 0)
        tally = tally.get()[...]
        named = jnp.zeros((LANES, pairs), F32)
        where = jnp.zeros((LANES, pairs), F32)
        for c in range(slots):
            hit = jnp.logical_and(parent_ref[c : c + 1, :] == line, tally > c)
            named = jnp.where(hit, 1.0, named)
            where = jnp.where(hit, place_ref[c : c + 1, :].astype(F32), where)
        before = (iota((pairs, pairs), 0) < iota((pairs, pairs), 1)).astype(F32).astype(BF16)
        rank_t = jnp.where(named > 0, mm(named.astype(BF16), before), -1.0)
        own_rank, own_place = rank_t[0:owners], where[0:owners]
        lane = iota((owners, LANES), 1)
        asks = jnp.zeros((owners, LANES), F32)
        for p in range(cap):
            row = jnp.sum(jnp.where(own_rank == p, own_place, 0.0), axis=1, keepdims=True)
            asks = jnp.where(lane == p, row, asks)
        asks = asks.astype(jnp.int32)
        for o in range(owners):
            ask.stage[o] = jnp.broadcast_to(asks[o : o + 1, :], ask.stage.shape[1:])
        ask.start()
        rank_t_ref[...] = rank_t.astype(BF16)
        rank_ref[...] = rank_t.T.astype(BF16)
        ask.finish()

    return kernel


def narrow(table, out_ref):
    out_ref[...] = table.get()[...].astype(BF16)


def normalize(rows):
    radius = jnp.sqrt(jnp.sum(rows * rows, axis=1, keepdims=True) + epsilon)
    return rows / radius, radius


def unit_queries(query, lines, send_ref):
    query_ref, lines_ref = query.get(), lines.get()
    pairs = query_ref.shape[0]
    slots = lines_ref.shape[0]
    unit, _ = normalize(query_ref[...].astype(F32))
    send_ref[0:pairs, :] = unit.astype(BF16)
    tail = send_ref.shape[0] - pairs
    line = iota((tail, pairs), 0)
    extra = jnp.zeros((tail, pairs), F32)
    for h in range(slots):
        row = lines_ref[h : h + 1, :]
        extra = jnp.where(line == h, (row // 64).astype(F32), extra)
        extra = jnp.where(line == h + slots, (row % 64).astype(F32), extra)
    send_ref[pairs:, :] = extra.astype(BF16)


def prepare(cap):
    def kernel(rank_ref, rank_t_ref, lines, hot, pick_ref, placed, hot_sum_ref):
        lines_ref = lines.get()
        pairs = rank_ref.shape[0]
        slots = lines_ref.shape[0]
        rank, rank_t = rank_ref[...], rank_t_ref[...]
        line = iota((LANES, pairs), 0)
        lines = jnp.zeros((LANES, pairs), F32)
        for h in range(slots):
            lines = jnp.where(line == h, lines_ref[h : h + 1, :].astype(F32), lines)
        lines = lines.T.astype(jnp.int32)
        width = placed.width
        want = (iota((pairs, width), 1) % cap).astype(F32)
        want_t = (iota((width, pairs), 0) % cap).astype(F32)
        hot_ref = hot.get()
        hot_sum_ref[...] = jnp.zeros_like(hot_sum_ref)

        def compute(i):
            base = pl.multiple_of(i * width, width)
            spread = expander(LANES, cap, base, width)
            pick_ref[:, pl.ds(base, width)] = (mm(rank, spread) == want).astype(F32).astype(BF16)
            column = iota((pairs, width), 1) + base
            counts = jnp.zeros((pairs, width), F32)
            for h in range(slots):
                counts += (lines[:, h : h + 1] == column).astype(F32)
            hot_sum_ref[...] += mm(counts.astype(BF16), hot_ref[pl.ds(base, width), :])
            spread_t = ((iota((width, LANES), 0) + base) // cap == iota((width, LANES), 1))
            hit = mm(spread_t.astype(F32).astype(BF16), rank_t) == want_t
            return hit.astype(F32).astype(BF16)

        placed.run(compute)

    return kernel


def fetch(ask_ref, table_ref, out, column_ref):
    rows = table_ref.shape[0]
    owners, cap, _ = out.stage.shape
    group = out.width
    asks = [ask_ref[o, 0:1, :].astype(F32) for o in range(owners)]
    asks = jnp.concatenate(asks + [jnp.zeros((LANES - owners, LANES), F32)], axis=0).T.astype(jnp.int32)
    for o in range(owners):
        column_ref[o * cap : (o + 1) * cap, :] = asks[0:cap, o : o + 1]
    size = group * cap
    lane = iota((size, rows), 1).astype(jnp.int16)

    def compute(i):
        column = column_ref[pl.ds(i * size, size), :]
        column = jnp.broadcast_to(column, (size, LANES)).astype(jnp.int16)
        column = jnp.tile(column, (1, rows // LANES))
        hit = jnp.where(column == lane, jnp.ones((), BF16), jnp.zeros((), BF16))
        return mm(hit, table_ref[...]).astype(BF16).reshape(group, cap, table_ref.shape[1])

    out.run(compute)


def loss_side(own_low, others, own_at, sharpness, additive):
    rows = own_low.shape[0]
    others = [other[0:rows, :] for other in others]
    grads = []
    for i, other in enumerate(others):
        grad = jax.nn.sigmoid(sharpness * mm(own_low, other, NT) + additive)
        if i == own_at:
            grad = grad - (iota((rows, rows), 0) == iota((rows, rows), 1)).astype(F32)
        grads.append(grad.astype(BF16))
    return sharpness * mm(jnp.concatenate(grads, axis=1), jnp.concatenate(others, axis=0))


def project(unit, radius, direction):
    inner = jnp.sum(unit * direction, axis=1, keepdims=True)
    return (direction - unit * inner) / radius


def item_side(near, far):
    def kernel(sharp_ref, add_ref, fetched_ref, pick_ref, hot_sum_ref, *refs):
        near_refs, far_blocks, place = refs[:near], refs[near : near + far], refs[near + far]
        sides_ref, tails_ref, outgoing = refs[near + far + 1 :]
        pairs = hot_sum_ref.shape[0]
        unit, radius = normalize(mm(pick_ref[...], fetched_ref[...]) + hot_sum_ref[...])
        low = unit.astype(BF16)
        sides_ref[0:pairs, :] = low
        queries = list(near_refs) + [block.get() for block in far_blocks]
        for i, ref in enumerate(queries):
            tails_ref[i] = ref[pairs:, :]
        direction = loss_side(low, queries, near + far - 1, sharp_ref[0], add_ref[0])
        grad = project(unit, radius, direction).astype(BF16)
        sides_ref[pairs:, :] = grad
        place_ref = place.get()
        width = outgoing.width
        outgoing.run(lambda i: mm(place_ref[pl.ds(i * width, width), :], grad).astype(BF16))

    return kernel


def query_side(sharp_ref, add_ref, query, *refs):
    item_refs, out = refs[:-1], refs[-1]
    unit, radius = normalize(query.get()[...].astype(F32))
    direction = loss_side(unit.astype(BF16), item_refs, 0, sharp_ref[0], add_ref[0])
    out.write(project(unit, radius, direction))
    out.finish()


def hot_terms(blocks, slots):
    def kernel(block_ref, lines_ref, *refs):
        side_refs, (out, total_ref) = refs[:blocks], refs[blocks:]
        width, pairs = total_ref.shape
        row = (iota((width, pairs), 0) + block_ref[0] * width).astype(F32)
        for i, ref in enumerate(side_refs):
            line = lines_ref[i].astype(F32)
            counts = jnp.zeros((width, pairs), F32)
            for h in range(slots):
                counts += (line[h : h + 1, :] * 64.0 + line[h + slots : h + slots + 1, :] == row).astype(F32)
            term = mm(counts.astype(BF16), ref[pairs:, :])
            total_ref[...] = term if i == 0 else total_ref[...] + term
        out.write(total_ref[...].astype(BF16))
        out.finish()

    return kernel


def hot_sum_spread(parts_ref, out):
    piece = jnp.sum(parts_ref[...].astype(F32), axis=0, keepdims=True)
    out.write(jnp.broadcast_to(piece, parts_ref.shape).astype(BF16))
    out.finish()


def widen(blocks):
    def kernel(block_ref, *refs):
        part_refs, out = refs[:blocks], refs[blocks]
        chips = blocks // 2
        width = part_refs[0].shape[0]
        mine, core = block_ref[0] // 2, block_ref[0] % 2
        copies = []
        for i, ref in enumerate(part_refs):
            chip = (mine + chips - i % chips) % chips
            index = chip * 2 + (core if i < chips else 1 - core)
            part = pl.ds(i * width, width)
            out.stage[part, :] = ref[...].astype(F32)
            place = pl.ds(pl.multiple_of(index * width, width), width)
            copies.append(pltpu.make_async_copy(out.stage.at[part], out.out.at[place], out.sem.at[i]))
            copies[-1].start()
        for copy in copies:
            copy.wait()

    return kernel


def cold_terms(same_core):
    def kernel(block_ref, ask_ref, grad_ref, out_ref, row_ref):
        chips, width, _ = out_ref.shape
        total = grad_ref.shape[0]
        owners = ask_ref.shape[0]
        cap = total // owners
        for o in range(owners):
            row_ref[:, o * cap : (o + 1) * cap] = ask_ref[o, 0:1, 0:cap]
        core = block_ref[0] % 2
        core = core if same_core else 1 - core

        def step(i, _):
            chip = (block_ref[0] // 2 + i) % chips
            row = iota((width, total), 0) + (chip * 2 + core) * width
            hit = (row_ref[...] == row).astype(F32).astype(BF16)
            out_ref[i] = mm(hit, grad_ref[...]).astype(out_ref.dtype)
            return 0

        lax.fori_loop(0, chips, step, 0)

    return kernel


def cold_join(mine_ref, theirs_ref, keep_ref, *send_refs):
    keep_ref[...] = mine_ref[0] + theirs_ref[0].astype(F32)
    for d, ref in enumerate(send_refs):
        ref[...] = (mine_ref[d + 1] + theirs_ref[d + 1].astype(F32)).astype(BF16)


def add_parts(keep_ref, *refs):
    part_refs, out = refs[:-1], refs[-1]
    total = keep_ref[...]
    for ref in part_refs:
        total += ref[...].astype(F32)
    out.write(total)
    out.finish()


def swap(array, axis):
    return lax.all_to_all(array, axis, split_axis=0, concat_axis=0, tiled=True)


def cross(array, blocks):
    return lax.ppermute(array, "blk", [(i, i ^ 1) for i in range(blocks)])


def shift(array, blocks, d):
    return lax.ppermute(array, "blk", [(i, (i + 2 * d) % blocks) for i in range(blocks)])


def gather_blocks(array, blocks):
    first = cross(array, blocks)
    mine = []
    for d in range(1, blocks // 2):
        mine.append(shift(array, blocks, d))
    return [array] + mine + [first] + [cross(m, blocks) for m in mine]


def step_of(queries, hot_table, cold_table, lines, parent, place, tally, sharpness, additive):
    pairs, width = queries.shape
    owners, blocks = lax.axis_size("shard"), lax.axis_size("blk")
    chips = blocks // 2
    slots = parent.shape[1]
    cap = 2 * pairs * slots // owners
    total = owners * cap
    rows = cold_table.shape[0]
    hot_rows = hot_table.shape[0]
    block = lax.axis_index("blk").astype(jnp.int32).reshape(1)

    rank, rank_t, ask = call(
        make_requests(owners, cap),
        [shape((pairs, LANES), BF16), shape((LANES, pairs), BF16), HBM((owners, 8, LANES), jnp.int32)],
        parent.T, place.T, tally.reshape(1, pairs),
        kinds=["h"] * 3,
        flops=2 * pairs * pairs * LANES,
    )
    (table_low,) = call(narrow, [shape((rows, width), BF16)], cold_table, kinds=["h"])
    asked = swap(ask, "shard")

    steps = 8
    (looked,) = call(
        fetch,
        [HBM((owners, cap, width), BF16)],
        asked, table_low,
        scratch=[pltpu.VMEM((total, 1), jnp.int32)],
        steps=4,
        flops=2 * total * rows * width,
    )
    looked, queries, rank, rank_t = lax.optimization_barrier((looked, queries, rank, rank_t))
    fetched = swap(looked, "shard").reshape(total, width)

    lines_t = lines.T
    (query_block,) = call(unit_queries, [shape((pairs + 16, width), BF16)], queries, lines_t, kinds=["h", "h"])
    query_blocks = gather_blocks(query_block, blocks)

    pick, placed, hot_sum = call(
        prepare(cap),
        [shape((pairs, total), BF16), HBM((total, pairs), BF16), shape((pairs, width), F32)],
        rank, rank_t, lines_t, hot_table,
        kinds=["v", "v", "h", "h"],
        steps=steps,
        flops=2 * pairs * total * (width + 2 * LANES),
    )

    far = 3
    order = list(range(1, blocks)) + [0]
    sides, tails, outgoing = call(
        item_side(blocks - far, far),
        [shape((2 * pairs, width), BF16), shape((blocks, 16, width), BF16), HBM((total, width), BF16)],
        sharpness, additive, fetched, pick, hot_sum, *[query_blocks[i] for i in order], placed,
        kinds=["s", "s", "v", "v", "v"] + ["v"] * (blocks - far) + ["h"] * (far + 1),
        steps=steps,
        flops=2 * pairs * width * (2 * total + 2 * blocks * pairs),
    )
    incoming = swap(outgoing.reshape(owners, cap, width), "shard").reshape(total, width)

    side_blocks = gather_blocks(sides, blocks)
    (hot_block,) = call(
        hot_terms(blocks, slots),
        [HBM((hot_rows // blocks, width), BF16)],
        block, tails, *[side_blocks[i] for i in order],
        kinds=["s"] + ["v"] * (blocks + 1),
        scratch=[pltpu.VMEM((hot_rows // blocks, width), F32)],
        flops=2 * blocks * pairs * width * hot_rows // blocks,
    )
    (query_grad,) = call(
        query_side,
        [HBM((pairs, width), F32)],
        sharpness, additive, queries, *side_blocks,
        kinds=["s", "s", "h"] + ["v"] * blocks,
        flops=4 * pairs * width * blocks * pairs,
    )
    hot_parts = swap(hot_block.reshape(owners, hot_rows // blocks // owners, width), "shard")
    (hot_piece,) = call(hot_sum_spread, [HBM(hot_parts.shape, BF16)], hot_parts)

    def cold_half(same_core, dtype, incoming):
        return call(
            cold_terms(same_core),
            [shape((chips, rows // blocks, width), dtype)],
            block, asked, incoming,
            kinds=["s", "v", "v"],
            scratch=[pltpu.VMEM((1, total), jnp.int32)],
            flops=total * rows * width,
        )[0]

    theirs = cold_half(False, BF16, incoming)
    theirs = cross(theirs, blocks)
    mine = cold_half(True, F32, incoming)
    keep, *sends = call(
        cold_join,
        [shape((rows // blocks, width), F32)] + [shape((rows // blocks, width), BF16)] * (chips - 1),
        mine, theirs,
    )
    hot_block = swap(hot_piece, "shard").reshape(hot_rows // blocks, width)
    parts = [shift(part, blocks, d + 1) for d, part in enumerate(sends)]
    (cold_grad,) = call(add_parts, [HBM((rows // blocks, width), F32)], keep, *parts)
    hot_blocks = gather_blocks(hot_block, blocks)
    (hot_grad,) = call(
        widen(blocks),
        [HBM((hot_rows, width), F32)],
        block, *hot_blocks,
        kinds=["s"] + ["v"] * blocks,
        steps=blocks,
    )
    return (query_grad, hot_grad, cold_grad)


def solution(mesh):
    pair = P(("shard", "blk"), None)
    in_specs = (pair, P(), P("shard", None), pair, pair, pair, P(("shard", "blk")), P(), P())
    return jax.shard_map(step_of, mesh=mesh, in_specs=in_specs, out_specs=(pair, P(), pair), check_vma=False)
```

```python
import jax
import jax.numpy as jnp
from jax import lax
from jax.experimental import pallas as pl
from jax.experimental.pallas import tpu as pltpu
from jax.sharding import PartitionSpec as P


epsilon = 1e-06
F32 = jnp.float32
BF16 = jnp.bfloat16
NN = (((1,), (0,)), ((), ()))
NT = (((1,), (1,)), ((), ()))


def mm(a, b, dims=NN):
    return lax.dot_general(a, b, dims, preferred_element_type=F32)


def iota(shape, dim):
    return lax.broadcasted_iota(jnp.int32, shape, dim)


HBM = pltpu.HBM


class Late:
    def __init__(self, source, buffer, sem):
        self.copy = pltpu.make_async_copy(source, buffer, sem)
        self.buffer = buffer
        self.copy.start()
        self.waits = True

    def get(self):
        if self.waits:
            self.copy.wait()
            self.waits = False
        return self.buffer


class Leave:
    def __init__(self, out_ref, stage_ref, sem):
        self.out, self.stage, self.sem = out_ref, stage_ref, sem
        self.steps = sem.shape[0]
        self.width = stage_ref.shape[0] // self.steps

    def copy(self, i):
        part = pl.ds(i * self.width, self.width)
        return pltpu.make_async_copy(self.stage.at[part], self.out.at[part], self.sem.at[i])

    def write(self, value):
        self.stage[...] = value
        self.start()

    def start(self):
        for i in range(self.steps):
            self.copy(i).start()

    def finish(self):
        for i in range(self.steps):
            self.copy(i).wait()

    def run(self, compute):
        def step(i, _):
            self.stage[pl.ds(i * self.width, self.width)] = compute(i)
            self.copy(i).start()
            return 0

        def finish(i, _):
            self.copy(i).wait()
            return 0

        lax.fori_loop(0, self.steps, step, 0)
        lax.fori_loop(0, self.steps, finish, 0)


def call(kernel, outs, *args, kinds=None, scratch=(), flops=0, steps=1):
    kinds = kinds or ["v"] * len(args)
    late = [k for k, kind in enumerate(kinds) if kind == "h" or isinstance(kind, slice)]
    leaves = [k for k, out in enumerate(outs) if not isinstance(out, jax.ShapeDtypeStruct)]
    operands = [pltpu.with_memory_space_constraint(a, HBM) if k in late else a for k, a in enumerate(args)]
    spaces = [pltpu.SMEM if kind == "s" else HBM if k in late else pltpu.VMEM for k, kind in enumerate(kinds)]
    buffers = []
    for k in late:
        rows = args[k].shape[0] if kinds[k] == "h" else kinds[k].stop - kinds[k].start
        buffers += [pltpu.VMEM((rows,) + args[k].shape[1:], args[k].dtype), pltpu.SemaphoreType.DMA]
    for k in leaves:
        buffers += [pltpu.VMEM(outs[k].shape, outs[k].dtype), pltpu.SemaphoreType.DMA((steps,))]

    def run(*refs):
        refs, extra = list(refs[: len(refs) - len(buffers)]), list(refs[len(refs) - len(buffers) :])
        for k in late:
            source = refs[k] if kinds[k] == "h" else refs[k].at[kinds[k]]
            refs[k] = Late(source, extra.pop(0), extra.pop(0))
        for k in leaves:
            refs[len(args) + k] = Leave(refs[len(args) + k], extra.pop(0), extra.pop(0))
        kernel(*refs)

    moved = sum(a.size * a.dtype.itemsize for a in args)
    return pl.pallas_call(
        run,
        out_shape=list(outs),
        in_specs=[pl.BlockSpec(memory_space=space) for space in spaces],
        out_specs=[pl.BlockSpec(memory_space=HBM if k in leaves else pltpu.VMEM) for k in range(len(outs))],
        scratch_shapes=list(scratch) + buffers,
        compiler_params=pltpu.CompilerParams(vmem_limit_bytes=24 << 20),
        cost_estimate=pl.CostEstimate(flops=flops, bytes_accessed=moved, transcendentals=0),
    )(*operands)


def shape(dims, dtype):
    return jax.ShapeDtypeStruct(dims, dtype)


def expander(owners, cap, base, width):
    return ((iota((owners, width), 1) + base) // cap == iota((owners, width), 0)).astype(F32).astype(BF16)


LANES = 128


def make_requests(owners, cap):
    def kernel(parent, place, tally, rank_ref, rank_t_ref, ask):
        parent_ref, place_ref = parent.get(), place.get()
        slots, pairs = parent_ref.shape
        line = iota((LANES, pairs), 0)
        tally = tally.get()[...]
        named = jnp.zeros((LANES, pairs), F32)
        where = jnp.zeros((LANES, pairs), F32)
        for c in range(slots):
            hit = jnp.logical_and(parent_ref[c : c + 1, :] == line, tally > c)
            named = jnp.where(hit, 1.0, named)
            where = jnp.where(hit, place_ref[c : c + 1, :].astype(F32), where)
        before = (iota((pairs, pairs), 0) < iota((pairs, pairs), 1)).astype(F32).astype(BF16)
        rank_t = jnp.where(named > 0, mm(named.astype(BF16), before), -1.0)
        own_rank, own_place = rank_t[0:owners], where[0:owners]
        lane = iota((owners, LANES), 1)
        asks = jnp.zeros((owners, LANES), F32)
        for p in range(cap):
            row = jnp.sum(jnp.where(own_rank == p, own_place, 0.0), axis=1, keepdims=True)
            asks = jnp.where(lane == p, row, asks)
        asks = asks.astype(jnp.int32)
        for o in range(owners):
            ask.stage[o] = jnp.broadcast_to(asks[o : o + 1, :], ask.stage.shape[1:])
        ask.start()
        rank_t_ref[...] = rank_t.astype(BF16)
        rank_ref[...] = rank_t.T.astype(BF16)
        ask.finish()

    return kernel


def narrow(table, out_ref):
    out_ref[...] = table.get()[...].astype(BF16)


def normalize(rows):
    radius = jnp.sqrt(jnp.sum(rows * rows, axis=1, keepdims=True) + epsilon)
    return rows / radius, radius


def unit_queries(query, lines, send_ref):
    query_ref, lines_ref = query.get(), lines.get()
    pairs = query_ref.shape[0]
    slots = lines_ref.shape[0]
    unit, _ = normalize(query_ref[...].astype(F32))
    send_ref[0:pairs, :] = unit.astype(BF16)
    tail = send_ref.shape[0] - pairs
    line = iota((tail, pairs), 0)
    extra = jnp.zeros((tail, pairs), F32)
    for h in range(slots):
        row = lines_ref[h : h + 1, :]
        extra = jnp.where(line == h, (row // 64).astype(F32), extra)
        extra = jnp.where(line == h + slots, (row % 64).astype(F32), extra)
    send_ref[pairs:, :] = extra.astype(BF16)


def prepare(cap):
    def kernel(rank_ref, rank_t_ref, lines, hot, pick_ref, placed, hot_sum_ref):
        lines_ref = lines.get()
        pairs = rank_ref.shape[0]
        slots = lines_ref.shape[0]
        rank, rank_t = rank_ref[...], rank_t_ref[...]
        line = iota((LANES, pairs), 0)
        lines = jnp.zeros((LANES, pairs), F32)
        for h in range(slots):
            lines = jnp.where(line == h, lines_ref[h : h + 1, :].astype(F32), lines)
        lines = lines.T.astype(jnp.int32)
        width = placed.width
        want = (iota((pairs, width), 1) % cap).astype(F32)
        want_t = (iota((width, pairs), 0) % cap).astype(F32)
        hot_ref = hot.get()
        hot_sum_ref[...] = jnp.zeros_like(hot_sum_ref)

        def compute(i):
            base = pl.multiple_of(i * width, width)
            spread = expander(LANES, cap, base, width)
            pick_ref[:, pl.ds(base, width)] = (mm(rank, spread) == want).astype(F32).astype(BF16)
            column = iota((pairs, width), 1) + base
            counts = jnp.zeros((pairs, width), F32)
            for h in range(slots):
                counts += (lines[:, h : h + 1] == column).astype(F32)
            hot_sum_ref[...] += mm(counts.astype(BF16), hot_ref[pl.ds(base, width), :])
            spread_t = ((iota((width, LANES), 0) + base) // cap == iota((width, LANES), 1))
            hit = mm(spread_t.astype(F32).astype(BF16), rank_t) == want_t
            return hit.astype(F32).astype(BF16)

        placed.run(compute)

    return kernel


def fetch(ask_ref, table_ref, out, column_ref):
    rows = table_ref.shape[0]
    owners, cap, _ = out.stage.shape
    group = out.width
    asks = [ask_ref[o, 0:1, :].astype(F32) for o in range(owners)]
    asks = jnp.concatenate(asks + [jnp.zeros((LANES - owners, LANES), F32)], axis=0).T.astype(jnp.int32)
    for o in range(owners):
        column_ref[o * cap : (o + 1) * cap, :] = asks[0:cap, o : o + 1]
    size = group * cap
    lane = iota((size, rows), 1).astype(jnp.int16)

    def compute(i):
        column = column_ref[pl.ds(i * size, size), :]
        column = jnp.broadcast_to(column, (size, LANES)).astype(jnp.int16)
        column = jnp.tile(column, (1, rows // LANES))
        hit = jnp.where(column == lane, jnp.ones((), BF16), jnp.zeros((), BF16))
        return mm(hit, table_ref[...]).astype(BF16).reshape(group, cap, table_ref.shape[1])

    out.run(compute)


def loss_side(own_low, others, own_at, sharpness, additive):
    rows = own_low.shape[0]
    others = [other[0:rows, :] for other in others]
    grads = []
    for i, other in enumerate(others):
        grad = jax.nn.sigmoid(sharpness * mm(own_low, other, NT) + additive)
        if i == own_at:
            grad = grad - (iota((rows, rows), 0) == iota((rows, rows), 1)).astype(F32)
        grads.append(grad.astype(BF16))
    return sharpness * mm(jnp.concatenate(grads, axis=1), jnp.concatenate(others, axis=0))


def project(unit, radius, direction):
    inner = jnp.sum(unit * direction, axis=1, keepdims=True)
    return (direction - unit * inner) / radius


def item_side(near, far):
    def kernel(sharp_ref, add_ref, fetched_ref, pick_ref, hot_sum_ref, *refs):
        near_refs, far_blocks, place = refs[:near], refs[near : near + far], refs[near + far]
        sides_ref, tails_ref, outgoing = refs[near + far + 1 :]
        pairs = hot_sum_ref.shape[0]
        unit, radius = normalize(mm(pick_ref[...], fetched_ref[...]) + hot_sum_ref[...])
        low = unit.astype(BF16)
        sides_ref[0:pairs, :] = low
        queries = list(near_refs) + [block.get() for block in far_blocks]
        for i, ref in enumerate(queries):
            tails_ref[i] = ref[pairs:, :]
        direction = loss_side(low, queries, near + far - 1, sharp_ref[0], add_ref[0])
        grad = project(unit, radius, direction).astype(BF16)
        sides_ref[pairs:, :] = grad
        place_ref = place.get()
        width = outgoing.width
        outgoing.run(lambda i: mm(place_ref[pl.ds(i * width, width), :], grad).astype(BF16))

    return kernel


def query_side(sharp_ref, add_ref, query, *refs):
    item_refs, out = refs[:-1], refs[-1]
    unit, radius = normalize(query.get()[...].astype(F32))
    direction = loss_side(unit.astype(BF16), item_refs, 0, sharp_ref[0], add_ref[0])
    out.write(project(unit, radius, direction))
    out.finish()


def hot_terms(blocks, slots):
    def kernel(block_ref, lines_ref, *refs):
        side_refs, (out, total_ref) = refs[:blocks], refs[blocks:]
        width, pairs = total_ref.shape
        row = (iota((width, pairs), 0) + block_ref[0] * width).astype(F32)
        for i, ref in enumerate(side_refs):
            line = lines_ref[i].astype(F32)
            counts = jnp.zeros((width, pairs), F32)
            for h in range(slots):
                counts += (line[h : h + 1, :] * 64.0 + line[h + slots : h + slots + 1, :] == row).astype(F32)
            term = mm(counts.astype(BF16), ref[pairs:, :])
            total_ref[...] = term if i == 0 else total_ref[...] + term
        out.write(total_ref[...].astype(BF16))
        out.finish()

    return kernel


def hot_sum_spread(parts_ref, out):
    piece = jnp.sum(parts_ref[...].astype(F32), axis=0, keepdims=True)
    out.write(jnp.broadcast_to(piece, parts_ref.shape).astype(BF16))
    out.finish()


def widen(blocks):
    def kernel(block_ref, *refs):
        part_refs, out = refs[:blocks], refs[blocks]
        chips = blocks // 2
        width = part_refs[0].shape[0]
        mine, core = block_ref[0] // 2, block_ref[0] % 2
        copies = []
        for i, ref in enumerate(part_refs):
            chip = (mine + chips - i % chips) % chips
            index = chip * 2 + (core if i < chips else 1 - core)
            part = pl.ds(i * width, width)
            out.stage[part, :] = ref[...].astype(F32)
            place = pl.ds(pl.multiple_of(index * width, width), width)
            copies.append(pltpu.make_async_copy(out.stage.at[part], out.out.at[place], out.sem.at[i]))
            copies[-1].start()
        for copy in copies:
            copy.wait()

    return kernel


def cold_terms(same_core):
    def kernel(block_ref, ask_ref, grad_ref, out_ref, row_ref):
        chips, width, _ = out_ref.shape
        total = grad_ref.shape[0]
        owners = ask_ref.shape[0]
        cap = total // owners
        for o in range(owners):
            row_ref[:, o * cap : (o + 1) * cap] = ask_ref[o, 0:1, 0:cap]
        core = block_ref[0] % 2
        core = core if same_core else 1 - core

        def step(i, _):
            chip = (block_ref[0] // 2 + i) % chips
            row = iota((width, total), 0) + (chip * 2 + core) * width
            hit = (row_ref[...] == row).astype(F32).astype(BF16)
            out_ref[i] = mm(hit, grad_ref[...]).astype(out_ref.dtype)
            return 0

        lax.fori_loop(0, chips, step, 0)

    return kernel


def cold_join(mine_ref, theirs_ref, keep_ref, *send_refs):
    keep_ref[...] = mine_ref[0] + theirs_ref[0].astype(F32)
    for d, ref in enumerate(send_refs):
        ref[...] = (mine_ref[d + 1] + theirs_ref[d + 1].astype(F32)).astype(BF16)


def add_parts(keep_ref, *refs):
    part_refs, out = refs[:-1], refs[-1]
    total = keep_ref[...]
    for ref in part_refs:
        total += ref[...].astype(F32)
    out.write(total)
    out.finish()


def swap(array, axis):
    return lax.all_to_all(array, axis, split_axis=0, concat_axis=0, tiled=True)


def cross(array, blocks):
    return lax.ppermute(array, "blk", [(i, i ^ 1) for i in range(blocks)])


def shift(array, blocks, d):
    return lax.ppermute(array, "blk", [(i, (i + 2 * d) % blocks) for i in range(blocks)])


def gather_blocks(array, blocks):
    first = cross(array, blocks)
    mine = [shift(array, blocks, d) for d in range(1, blocks // 2)]
    return [array] + mine + [first] + [cross(m, blocks) for m in mine]


def step_of(queries, hot_table, cold_table, lines, parent, place, tally, sharpness, additive):
    pairs, width = queries.shape
    owners, blocks = lax.axis_size("shard"), lax.axis_size("blk")
    chips = blocks // 2
    slots = parent.shape[1]
    cap = 2 * pairs * slots // owners
    total = owners * cap
    rows = cold_table.shape[0]
    hot_rows = hot_table.shape[0]
    block = lax.axis_index("blk").astype(jnp.int32).reshape(1)

    rank, rank_t, ask = call(
        make_requests(owners, cap),
        [shape((pairs, LANES), BF16), shape((LANES, pairs), BF16), HBM((owners, 8, LANES), jnp.int32)],
        parent.T, place.T, tally.reshape(1, pairs),
        kinds=["h"] * 3,
        flops=2 * pairs * pairs * LANES,
    )
    (table_low,) = call(narrow, [shape((rows, width), BF16)], cold_table, kinds=["h"])
    asked = swap(ask, "shard")

    steps = 8
    (looked,) = call(
        fetch,
        [HBM((owners, cap, width), BF16)],
        asked, table_low,
        scratch=[pltpu.VMEM((total, 1), jnp.int32)],
        steps=4,
        flops=2 * total * rows * width,
    )
    looked, queries, rank, rank_t = lax.optimization_barrier((looked, queries, rank, rank_t))
    fetched = swap(looked, "shard").reshape(total, width)

    lines_t = lines.T
    (query_block,) = call(unit_queries, [shape((pairs + 16, width), BF16)], queries, lines_t, kinds=["h", "h"])
    query_blocks = gather_blocks(query_block, blocks)

    pick, placed, hot_sum = call(
        prepare(cap),
        [shape((pairs, total), BF16), HBM((total, pairs), BF16), shape((pairs, width), F32)],
        rank, rank_t, lines_t, hot_table,
        kinds=["v", "v", "h", "h"],
        steps=steps,
        flops=2 * pairs * total * (width + 2 * LANES),
    )

    far = 3
    order = list(range(1, blocks)) + [0]
    sides, tails, outgoing = call(
        item_side(blocks - far, far),
        [shape((2 * pairs, width), BF16), shape((blocks, 16, width), BF16), HBM((total, width), BF16)],
        sharpness, additive, fetched, pick, hot_sum, *[query_blocks[i] for i in order], placed,
        kinds=["s", "s", "v", "v", "v"] + ["v"] * (blocks - far) + ["h"] * (far + 1),
        steps=4,
        flops=2 * pairs * width * (2 * total + 2 * blocks * pairs),
    )
    incoming = swap(outgoing.reshape(owners, cap, width), "shard").reshape(total, width)

    side_blocks = gather_blocks(sides, blocks)
    (hot_block,) = call(
        hot_terms(blocks, slots),
        [HBM((hot_rows // blocks, width), BF16)],
        block, tails, *[side_blocks[i] for i in order],
        kinds=["s"] + ["v"] * (blocks + 1),
        scratch=[pltpu.VMEM((hot_rows // blocks, width), F32)],
        flops=2 * blocks * pairs * width * hot_rows // blocks,
    )
    (query_grad,) = call(
        query_side,
        [HBM((pairs, width), F32)],
        sharpness, additive, queries, *side_blocks,
        kinds=["s", "s", "h"] + ["v"] * blocks,
        flops=4 * pairs * width * blocks * pairs,
    )
    hot_parts = swap(hot_block.reshape(owners, hot_rows // blocks // owners, width), "shard")
    (hot_piece,) = call(hot_sum_spread, [HBM(hot_parts.shape, BF16)], hot_parts)

    def cold_half(same_core, dtype, incoming):
        return call(
            cold_terms(same_core),
            [shape((chips, rows // blocks, width), dtype)],
            block, asked, incoming,
            kinds=["s", "v", "v"],
            scratch=[pltpu.VMEM((1, total), jnp.int32)],
            flops=total * rows * width,
        )[0]

    theirs = cold_half(False, BF16, incoming)
    theirs = cross(theirs, blocks)
    mine = cold_half(True, F32, incoming)
    keep, *sends = call(
        cold_join,
        [shape((rows // blocks, width), F32)] + [shape((rows // blocks, width), BF16)] * (chips - 1),
        mine, theirs,
    )
    hot_block = swap(hot_piece, "shard").reshape(hot_rows // blocks, width)
    parts = [shift(part, blocks, d + 1) for d, part in enumerate(sends)]
    (cold_grad,) = call(add_parts, [HBM((rows // blocks, width), F32)], keep, *parts)
    hot_blocks = gather_blocks(hot_block, blocks)
    (hot_grad,) = call(
        widen(blocks),
        [HBM((hot_rows, width), F32)],
        block, *hot_blocks,
        kinds=["s"] + ["v"] * blocks,
        steps=blocks,
    )
    return (query_grad, hot_grad, cold_grad)


def solution(mesh):
    pair = P(("shard", "blk"), None)
    in_specs = (pair, P(), P("shard", None), pair, pair, pair, P(("shard", "blk")), P(), P())
    return jax.shard_map(step_of, mesh=mesh, in_specs=in_specs, out_specs=(pair, P(), pair), check_vma=False)
```
